32 devices in a mesh: dp: 8 (over z, core), seq: 4 (over y, x).
Axes of the slice: x: 2, y: 2, z: 4, core: 2. Of those that a mesh axis runs over, the one named last changes fastest.
Arguments:
- hidden_in: bfloat16 [8, 512, 1024], P('dp', 'seq'), may hold values from -6 to 6
- doc_starts: int32 [8, 4], P('dp'), may hold values from 0 to 511, as said below
- w_query: bfloat16 [1024, 1024], P(('dp', 'seq')), may hold values from -0.25 to 0.25
- w_key: bfloat16 [1024, 1024], P(('dp', 'seq')), may hold values from -0.25 to 0.25
- w_value: bfloat16 [1024, 1024], P(('dp', 'seq')), may hold values from -0.1875 to 0.1875
- w_out: bfloat16 [1024, 1024], P(('dp', 'seq')), may hold values from -1 to 1
- w_gate: bfloat16 [1024, 2816], P(('dp', 'seq')), may hold values from -0.1875 to 0.1875
- w_up: bfloat16 [1024, 2816], P(('dp', 'seq')), may hold values from -0.1875 to 0.1875
- w_down: bfloat16 [2816, 1024], P(('dp', 'seq')), may hold values from -0.109375 to 0.109375
- out_grad: bfloat16 [8, 512, 1024], P('dp', 'seq'), may hold values from -6 to 6
Outputs:
- hidden_out: bfloat16 [8, 512, 1024], P('dp', 'seq')
- in_grad: float32 [8, 512, 1024], P('dp', 'seq')
- grad_query: float32 [1024, 1024], P(('dp', 'seq'))
- grad_key: float32 [1024, 1024], P(('dp', 'seq'))
- grad_value: float32 [1024, 1024], P(('dp', 'seq'))
- grad_out: float32 [1024, 1024], P(('dp', 'seq'))
- grad_gate: float32 [1024, 2816], P(('dp', 'seq'))
- grad_up: float32 [1024, 2816], P(('dp', 'seq'))
- grad_down: float32 [2816, 1024], P(('dp', 'seq'))
The draws below stay inside these ranges and needn't reach their ends.
Inputs may be any that keep to these rules, and one draw needn't show every extreme that they name: `doc_starts`: each row begins with 0 and rises strictly; documents run from one start to the next, the last to the stream's end, and may span devices.
All inputs are finite; a program needn't handle non-finite values.
Results may differ from the reference program's by a relative error of at most 0.014.
The reference program's roundings to bfloat16 on the way count: a program that leaves them out, or rounds other values in their place, can miss the bound.
Values may be sent and summed in bfloat16 or wider, within the bound.
No kernel may reach another device: no remote copies, remote signals or barrier semaphores. Data moves between devices by JAX's collectives and lax.ppermute only.
A program may use at most 128 MiB of HBM per device.

```python
import jax
import jax.numpy as jnp
from jax import lax

D = 1024
HEADS = 16
HEAD_DIM = 64
FF = 2816
NDOCS = 4
STREAMS = 8
SEQ_LEN = 512


def draw_doc_starts(key, part):
    keys = jax.random.split(jax.random.fold_in(key, 7), STREAMS)
    picks = jax.vmap(lambda sub_key: jax.random.permutation(sub_key, SEQ_LEN - 1)[:NDOCS - 1])(keys) + 1
    ordered = jnp.sort(picks.astype(jnp.int32), axis=1)
    ordered = ordered.at[0, NDOCS - 2].set(SEQ_LEN - 1)
    return jnp.concatenate([jnp.zeros((STREAMS, 1), jnp.int32), ordered], axis=1)


def shard_levels(key, dims, shards, low, largest):
    def one(dim, shards_of):
        draws = jax.random.uniform(jax.random.fold_in(jax.random.fold_in(key, 6), dim), (shards_of,), jnp.float32, low / len(shards), largest / len(shards))
        return jnp.repeat(jnp.exp(draws), dims[dim] // shards_of).reshape((-1,) + (1,) * (len(dims) - dim - 1))

    factor_of = one(*shards[0])
    for cut in shards[1:]:
        factor_of = factor_of * one(*cut)
    return factor_of


def normal_values(rng, extent, scale, most, cuts=(), kind=jnp.bfloat16):
    factor_of = shard_levels(rng, extent, cuts, -0.22, 0.18) if cuts else 1.0
    values = jax.random.normal(rng, extent, jnp.float32) * scale * factor_of
    return jnp.minimum(jnp.maximum(values, -most), most).astype(kind)


def setup_inputs(seed: int = 0) -> dict:
    seeds = jax.random.split(jax.random.key(seed), 11)
    hidden_in = normal_values(seeds[0], (STREAMS, SEQ_LEN, D), 1.0, 6.0, ((0, 8), (1, 4)))
    doc_starts = draw_doc_starts(jax.random.fold_in(seeds[10], 71), 0)
    w_query = normal_values(seeds[2], (D, D), (D // 2) ** -0.5, 0.25, ((0, 32),))
    w_key = normal_values(seeds[3], (D, D), (D // 2) ** -0.5, 0.25, ((0, 32),))
    w_value = normal_values(seeds[4], (D, D), D ** -0.5, 0.1875, ((0, 32),))
    w_out = normal_values(seeds[5], (D, D), (D // 32) ** -0.5, 1.0, ((0, 32),))
    w_gate = normal_values(seeds[6], (D, FF), D ** -0.5, 0.1875, ((0, 32),))
    w_up = normal_values(seeds[7], (D, FF), D ** -0.5, 0.1875, ((0, 32),))
    w_down = normal_values(seeds[8], (FF, D), FF ** -0.5, 0.109375, ((0, 32),))
    out_grad = normal_values(seeds[9], (STREAMS, SEQ_LEN, D), 1.0, 6.0, ((0, 8), (1, 4)))
    return dict(hidden_in=hidden_in, doc_starts=doc_starts, w_query=w_query, w_key=w_key, w_value=w_value, w_out=w_out, w_gate=w_gate, w_up=w_up, w_down=w_down, out_grad=out_grad)


@jax.custom_vjp
def low(v):
    return lax.optimization_barrier(v.astype(jnp.bfloat16)).astype(jnp.float32)

@jax.custom_vjp
def low_back(v):
    return v

def low_keep(v):
    return (low(v), None)

def low_pass(kept, grad):
    return (grad,)

def back_keep(v):
    return (v, None)

def back_low(kept, grad):
    return (low(grad),)
low.defvjp(low_keep, low_pass)
low_back.defvjp(back_keep, back_low)
eps = 1e-05

def matmul(left, right):
    return jnp.dot(left, right, precision=lax.Precision.HIGHEST)

def layer_norm(values):
    centred = values - lax.optimization_barrier(jnp.mean(values, axis=-1, keepdims=True))
    return centred * lax.rsqrt(lax.optimization_barrier(jnp.mean(centred * centred, axis=-1, keepdims=True)) + eps)

def rotary(values, positions):
    half = values.shape[-1] // 2
    freq = 10000.0 ** (-(jnp.arange(half, dtype=jnp.float32) * 2.0) / values.shape[-1])
    angle = positions.astype(jnp.float32)[:, None] * freq[None, :]
    cosine = jnp.cos(angle)[:, None, :]
    sine = jnp.sin(angle)[:, None, :]
    first = values[..., :half]
    second = values[..., half:]
    return jnp.concatenate([first * cosine - second * sine, second * cosine + first * sine], axis=-1)

def attention(queries, keys, values, segment, positions):
    length = queries.shape[0]
    block = 512 if length % 512 == 0 else length
    block_count = length // block
    scale = HEAD_DIM ** (-0.5)

    def one_block(item):
        query_blk, seg_query, pos_query = item
        scores = low_back(jnp.einsum('qhd,khd->hqk', query_blk, keys, precision=lax.Precision.HIGHEST) * scale)
        allowed = (seg_query[:, None] == segment[None, :]) & (positions[None, :] <= pos_query[:, None])
        scores = jnp.where(allowed[None], scores, -1e+30)
        top = lax.optimization_barrier(jnp.max(scores, axis=-1, keepdims=True))
        expo = jnp.exp(scores - top)
        probs = expo / lax.optimization_barrier(jnp.sum(expo, axis=-1, keepdims=True))
        return jnp.einsum('hqk,khd->qhd', low(probs), values, precision=lax.Precision.HIGHEST)
    result = lax.map(jax.checkpoint(one_block), (queries.reshape(block_count, block, HEADS, HEAD_DIM), segment.reshape(block_count, block), positions.reshape(block_count, block)))
    return result.reshape(length, HEADS, HEAD_DIM)

def stream_forward(inputs, starts, w_query, w_key, w_value, w_out, w_gate, w_up, w_down):
    length = inputs.shape[0]
    positions = jnp.arange(length, dtype=jnp.int32)
    segment = lax.optimization_barrier(jnp.sum((starts[None, :] <= positions[:, None]).astype(jnp.int32), axis=1))
    normed = low(layer_norm(inputs))
    q_pre = low_back(matmul(normed, w_query)).reshape(length, HEADS, HEAD_DIM)
    k_pre = low_back(matmul(normed, w_key)).reshape(length, HEADS, HEAD_DIM)
    queries = low_back(low(rotary(q_pre, positions)))
    keys = low_back(low(rotary(k_pre, positions)))
    values = low_back(low(matmul(normed, w_value))).reshape(length, HEADS, HEAD_DIM)
    context = attention(queries, keys, values, segment, positions).reshape(length, D)
    context = low_back(low(context))
    resid = inputs + low_back(matmul(context, w_out))
    normed2 = low(layer_norm(resid))
    gate = low_back(matmul(normed2, w_gate))
    up = low_back(matmul(normed2, w_up))
    hidden = low(jax.nn.silu(gate) * up)
    return resid + low_back(matmul(hidden, w_down))

def reference(hidden_in, doc_starts, w_query, w_key, w_value, w_out, w_gate, w_up, w_down, out_grad):
    weights = (w_query.astype(jnp.float32), w_key.astype(jnp.float32), w_value.astype(jnp.float32), w_out.astype(jnp.float32), w_gate.astype(jnp.float32), w_up.astype(jnp.float32), w_down.astype(jnp.float32))
    inputs = hidden_in.astype(jnp.float32)

    def forward(stream_inputs, mats):

        def one_stream(carry, item):
            rows, starts = item
            return (carry, jax.checkpoint(stream_forward)(rows, starts, *mats))
        unused, outputs = lax.scan(one_stream, jnp.zeros((), jnp.float32), (stream_inputs, doc_starts))
        return outputs
    result, pull = jax.vjp(forward, inputs, weights)
    d_inputs, d_mats = pull(out_grad.astype(jnp.float32))
    return (result.astype(jnp.bfloat16), d_inputs, d_mats[0], d_mats[1], d_mats[2], d_mats[3], d_mats[4], d_mats[5], d_mats[6])
```

```python
import functools

import jax
import jax.numpy as jnp
from jax import lax
from jax.experimental import pallas as pl
from jax.experimental.pallas import tpu as pltpu
from jax.sharding import Mesh, PartitionSpec as P

HEADS = 16
HEAD_DIM = 64
eps = 1e-05
bf16 = jnp.bfloat16
f32 = jnp.float32
NN = (((1,), (0,)), ((), ()))
NT = (((1,), (1,)), ((), ()))
TN = (((0,), (0,)), ((), ()))


def dot(left, right, dims=NN):
    return lax.dot_general(left, right, dims, preferred_element_type=f32)


def rows(start, size):
    return pl.ds(pl.multiple_of(start, size), size)


def norm_parts(values):
    centred = values - jnp.mean(values, axis=-1, keepdims=True)
    inv = lax.rsqrt(jnp.mean(centred * centred, axis=-1, keepdims=True) + eps)
    return centred * inv, inv


def norm_back(normed, inv, grad):
    mean_grad = jnp.mean(grad, axis=-1, keepdims=True)
    mean_both = jnp.mean(grad * normed, axis=-1, keepdims=True)
    return (grad - mean_grad - normed * mean_both) * inv


def call(kernel, outs, args, scratch=(), flops=0, smem=1, name=None):
    vmem = pl.BlockSpec(memory_space=pltpu.VMEM)
    in_specs = [pl.BlockSpec(memory_space=pltpu.SMEM)] * smem + [vmem] * (len(args) - smem)
    moved = sum(a.size * a.dtype.itemsize for a in args) + sum(
        o.size * jnp.dtype(o.dtype).itemsize for o in outs
    )
    return pl.pallas_call(
        kernel,
        out_shape=outs,
        in_specs=in_specs,
        out_specs=[vmem] * len(outs),
        scratch_shapes=list(scratch),
        cost_estimate=pl.CostEstimate(flops=flops, bytes_accessed=moved, transcendentals=0),
        compiler_params=pltpu.CompilerParams(vmem_limit_bytes=60 * 1024 * 1024),
        name=name,
    )(*args)


def out(shape, dtype):
    return jax.ShapeDtypeStruct(shape, dtype)


def turn(values, cosine, sine, sign):
    width = values.shape[-1]
    half = HEAD_DIM // 2
    lane = lax.broadcasted_iota(jnp.int32, values.shape, 1)
    first = (lane & (HEAD_DIM - 1)) < half
    ahead = pltpu.roll(values, width - half, 1)
    behind = pltpu.roll(values, half, 1)
    other = jnp.where(first, -ahead, behind)
    return values * cosine + (other * sine if sign > 0 else -(other * sine))


def head_lanes(shape, head):
    lane = lax.broadcasted_iota(jnp.int32, shape, 1)
    return (lane >= head * HEAD_DIM) & (lane < (head + 1) * HEAD_DIM)


def masked(scores, starts, first_row):
    pos = lax.broadcasted_iota(jnp.int32, (scores.shape[0], 1), 0) + first_row
    begin = jnp.zeros_like(pos)
    for start in starts:
        begin = jnp.where(pos >= start, start, begin)
    keys = lax.broadcasted_iota(jnp.int32, scores.shape, 1)
    return jnp.where((keys >= begin) & (keys <= pos), scores, -1e30)


def attend_kernel(n, docs, info, *refs):
    xs = refs[:n]
    own, other, cos_ref, sin_ref = refs[n : n + 4]
    normed, mats, qkv, lse, context = refs[n + 4 :]
    j, c = info[0], info[2]
    tokens = xs[0].shape[0]
    for k in range(n):
        block, unused = norm_parts(xs[k][...].astype(f32))
        normed[rows((j ^ k) * tokens, tokens), :] = block.astype(bf16)
    planes, height = own.shape[0], own.shape[1]
    for z in range(planes):
        mats[rows((2 * z + c) * height, height), :] = own[z]
        mats[rows((2 * z + 1 - c) * height, height), :] = other[z]
    pre = dot(normed[...], mats[...])
    width = pre.shape[1] // 3
    reps = width // cos_ref.shape[1]
    cosine = jnp.concatenate([cos_ref[...]] * reps, axis=1)
    sine = jnp.concatenate([sin_ref[...]] * reps, axis=1)
    qkv[:, :width] = (
        turn(pre[:, :width], cosine, sine, 1).astype(bf16).astype(f32) * HEAD_DIM**-0.5
    ).astype(bf16)
    qkv[:, width : 2 * width] = turn(pre[:, width : 2 * width], cosine, sine, 1).astype(bf16)
    qkv[:, 2 * width :] = pre[:, 2 * width :].astype(bf16)
    starts = [info[3 + d] for d in range(docs)]
    length = qkv.shape[0]
    step = 256

    def some_rows(b, carry):
        here = rows(b * step, step)
        query = qkv[here, :width]
        total = jnp.zeros((step, width), f32)
        for head in range(width // HEAD_DIM):
            mine = head_lanes(query.shape, head)
            scores = dot(jnp.where(mine, query, 0), qkv[:, width : 2 * width], NT)
            scores = masked(scores, starts, b * step)
            top = jnp.max(scores, axis=-1, keepdims=True)
            expo = jnp.exp(scores - top)
            mass = jnp.sum(expo, axis=-1, keepdims=True)
            probs = (expo * (1.0 / mass)).astype(bf16)
            total = jnp.where(mine, dot(probs, qkv[:, 2 * width :]), total)
            lse[here, head : head + 1] = top + jnp.log(mass)
        context[here, :] = total.astype(bf16)
        return carry

    lax.fori_loop(0, length // step, some_rows, 0)


def project_kernel(n, info, *refs):
    contexts = refs[:n]
    mats = refs[n]
    xs = refs[n + 1 : 2 * n + 1]
    resid_own, normed, mine, acc = refs[2 * n + 1 :]
    j = info[0]
    width = contexts[0].shape[1]
    tokens = xs[0].shape[0]
    acc[...] = dot(contexts[0][...], mats[rows(j * width, width), :])
    for p in range(1, n):
        acc[...] += dot(contexts[p][...], mats[rows((j ^ p) * width, width), :])
    mine[...] = mats[rows(j * width, width), :]
    for k in range(n):
        here = rows((j ^ k) * tokens, tokens)
        resid = xs[k][...].astype(f32) + acc[here, :]
        if k == 0:
            resid_own[...] = resid
        normed[here, :] = norm_parts(resid)[0].astype(bf16)


def ffn_kernel(n, planes, info, normed, *refs):
    gu = refs[: 2 * planes]
    down = refs[2 * planes : 4 * planes]
    grads = refs[4 * planes : 4 * planes + n]
    hidden, d_gu, own_grad, *rest = refs[4 * planes + n :]
    sends = rest[: n - 1]
    down_mat, og_full, gu_mat, acc = rest[n - 1 :]
    j, z, c = info[0], info[1], info[2]
    tokens = grads[0].shape[0]
    height = gu[0].shape[0]
    rows_in = down[0].shape[0]
    slot = down_mat.shape[0] // (2 * planes)
    if slot > rows_in:
        down_mat[...] = jnp.zeros_like(down_mat)
    for k in range(planes):
        for m in range(2):
            block = 2 * (z ^ k) + (c ^ m)
            gu_mat[rows(block * height, height), :] = gu[2 * k + m][...]
            down_mat[pl.ds(pl.multiple_of(block * slot, slot), rows_in), :] = down[2 * k + m][...]
    for k in range(n):
        og_full[rows((j ^ k) * tokens, tokens), :] = grads[k][...]
    width = hidden.shape[1]
    gate = dot(normed[...], gu_mat[:, :width])
    up = dot(normed[...], gu_mat[:, width:])
    d_hidden = dot(og_full[...], down_mat[...], NT)
    sig = 1.0 / (1.0 + jnp.exp(-gate))
    silu = gate * sig
    hidden[...] = (silu * up).astype(bf16)
    d_gu[:, :width] = (d_hidden * up * (sig + gate * sig * (1.0 - sig))).astype(bf16)
    d_gu[:, width:] = (d_hidden * silu).astype(bf16)
    acc[...] = dot(d_gu[...], gu_mat[...], NT)
    own_grad[...] = acc[rows(j * tokens, tokens), :]
    for k in range(1, n):
        sends[k - 1][...] = acc[rows((j ^ k) * tokens, tokens), :].astype(bf16)


def spread_kernel(n, info, left, right, own, *rest):
    sends = rest[: n - 1]
    acc = rest[n - 1]
    j = info[0]
    tokens = own.shape[0]
    acc[...] = dot(left[...], right[...])
    own[...] = acc[rows(j * tokens, tokens), :]
    for k in range(1, n):
        sends[k - 1][...] = acc[rows((j ^ k) * tokens, tokens), :].astype(bf16)


def resid_back_kernel(n, *refs):
    parts = refs[:n]
    resid, out_grad, d_resid, d_branch = refs[n:]
    grad = parts[0][...]
    for part in parts[1:]:
        grad = grad + part[...].astype(f32)
    normed, inv = norm_parts(resid[...])
    total = out_grad[...].astype(f32) + norm_back(normed, inv, grad)
    d_resid[...] = total
    d_branch[...] = total.astype(bf16)


def input_back_kernel(n, *refs):
    parts = refs[:n]
    x, d_resid, in_grad = refs[n:]
    grad = parts[0][...]
    for part in parts[1:]:
        grad = grad + part[...].astype(f32)
    normed, inv = norm_parts(x[...].astype(f32))
    in_grad[...] = d_resid[...] + norm_back(normed, inv, grad)


def attend_back_kernel(n, docs, info, *refs):
    branches = refs[:n]
    mine, qkv, lse, mats, cos_ref, sin_ref = refs[n : n + 6]
    d_qkv, db_full, own, *rest = refs[n + 6 :]
    sends = rest[: n - 1]
    d_key, d_value, d_query, acc = rest[n - 1 :]
    j = info[0]
    tokens = branches[0].shape[0]
    for k in range(n):
        db_full[rows((j ^ k) * tokens, tokens), :] = branches[k][...]
    length = qkv.shape[0]
    width = mine.shape[0]
    starts = [info[3 + d] for d in range(docs)]
    step = 256
    d_key[...] = jnp.zeros_like(d_key)
    d_value[...] = jnp.zeros_like(d_value)

    def some_rows(b, carry):
        here = rows(b * step, step)
        d_context = dot(db_full[here, :], mine[...], NT).astype(bf16)
        query = qkv[here, :width]
        d_q = jnp.zeros((step, width), f32)
        for head in range(width // HEAD_DIM):
            lanes = head_lanes(query.shape, head)
            q_head = jnp.where(lanes, query, 0)
            g_head = jnp.where(lanes, d_context, 0)
            keys = qkv[:, width : 2 * width]
            scores = dot(q_head, keys, NT)
            scores = masked(scores, starts, b * step)
            probs = jnp.exp(scores - lse[here, head : head + 1])
            d_probs = dot(g_head, qkv[:, 2 * width :], NT)
            delta = jnp.sum(probs * d_probs, axis=-1, keepdims=True)
            d_scores = (probs * (d_probs - delta)).astype(bf16)
            d_value[...] += dot(probs.astype(bf16), g_head, TN)
            d_key[...] += dot(d_scores, q_head, TN)
            d_q = jnp.where(lanes, dot(d_scores, keys), d_q)
        d_query[here, :] = d_q * HEAD_DIM**-0.5
        return carry

    lax.fori_loop(0, length // step, some_rows, 0)
    reps = width // cos_ref.shape[1]
    cosine = jnp.concatenate([cos_ref[...]] * reps, axis=1)
    sine = jnp.concatenate([sin_ref[...]] * reps, axis=1)
    low_q = d_query[...].astype(bf16).astype(f32)
    low_k = d_key[...].astype(bf16).astype(f32)
    d_qkv[:, :width] = turn(low_q, cosine, sine, -1).astype(bf16)
    d_qkv[:, width : 2 * width] = turn(low_k, cosine, sine, -1).astype(bf16)
    d_qkv[:, 2 * width :] = d_value[...].astype(bf16)
    acc[...] = dot(d_qkv[...], mats[...], NT)
    own[...] = acc[rows(j * tokens, tokens), :]
    for k in range(1, n):
        sends[k - 1][...] = acc[rows((j ^ k) * tokens, tokens), :].astype(bf16)


def grad_kernel(info, left, right, keep, send, acc):
    c = info[2]
    acc[...] = dot(left[...], right[...], TN)
    planes, height = keep.shape[0], keep.shape[1]
    slot = acc.shape[0] // (2 * planes)
    for z in range(planes):
        keep[z] = acc[pl.ds(pl.multiple_of((2 * z + c) * slot, slot), height), :]
        send[z] = acc[pl.ds(pl.multiple_of((2 * z + 1 - c) * slot, slot), height), :].astype(bf16)


def grad_out_kernel(n, info, *refs):
    contexts = refs[:n]
    right, keep, send, turned, left = refs[n:]
    j, c = info[0], info[2]
    width = contexts[0].shape[1]
    for p in range(n):
        turned[rows((j ^ p) * width, width), :] = contexts[p][...].astype(f32).T
    planes, height = keep.shape[0], keep.shape[1]
    block = height * n
    for m in range(2):
        for z in range(planes):
            at = (2 * z + (c ^ m)) * block + j * height
            left[pl.ds((m * planes + z) * height, height), :] = turned[
                pl.ds(pl.multiple_of(at, height), height), :
            ]
    product = dot(left[...].astype(bf16), right[...])
    for z in range(planes):
        keep[z] = product[z * height : (z + 1) * height]
        send[z] = product[(planes + z) * height : (planes + z + 1) * height].astype(bf16)


def body(hidden_in, doc_starts, w_query, w_key, w_value, w_out, w_gate, w_up, w_down, out_grad):
    x = hidden_in[0]
    og = out_grad[0]
    tokens, width = x.shape
    seq = ("seq_hi", "seq_lo")
    n = lax.axis_size(seq)
    planes = lax.axis_size("plane")
    length = tokens * n
    group = HEADS // n * HEAD_DIM
    docs = doc_starts.shape[1]
    j = lax.axis_index(seq)
    z = lax.axis_index("plane")
    c = lax.axis_index("core")
    info = jnp.concatenate([jnp.stack([j, z, c]).astype(jnp.int32), doc_starts[0]])

    def swap(a):
        return lax.ppermute(a, "core", [(0, 1), (1, 0)])

    def around(a, k):
        return lax.ppermute(a, seq, [(t, t ^ k) for t in range(n)])

    def across(a, k):
        return lax.ppermute(a, "plane", [(t, t ^ k) for t in range(planes)])

    def gather_seq(a):
        return [a] + [around(a, k) for k in range(1, n)]

    def gather_planes(a):
        return [a] + [across(a, k) for k in range(1, planes)]

    def natural(blocks, index):
        stacked = jnp.stack(blocks)
        return [
            lax.dynamic_index_in_dim(stacked, index ^ t, 0, keepdims=False)
            for t in range(len(blocks))
        ]

    def after(a, dep):
        return lax.optimization_barrier((a, dep))[0]

    def to_all(blocks):
        return lax.all_to_all(blocks, ("plane",) + seq, split_axis=0, concat_axis=0, tiled=True)

    half = HEAD_DIM // 2
    freq = 10000.0 ** (-(jnp.arange(half, dtype=f32) * 2.0) / HEAD_DIM)
    lane_freq = jnp.concatenate([freq] * (128 // half))
    angle = jnp.arange(length, dtype=f32)[:, None] * lane_freq[None, :]
    cosine, sine = jnp.cos(angle), jnp.sin(angle)

    height = w_query.shape[0]
    mats_in = jnp.stack([w_query, w_key, w_value]).reshape(3, height, n, group)
    mats_in = mats_in.transpose(2, 1, 0, 3).reshape(1, n, height, 3 * group)
    mats_in = jnp.broadcast_to(mats_in, (planes, n, height, 3 * group))
    qkv_own = to_all(mats_in.reshape(planes * n, height, 3 * group))
    qkv_own = qkv_own.reshape(planes, n * height, 3 * group)
    qkv_other = swap(qkv_own)
    xs = gather_seq(x)

    units = w_down.shape[0]
    slot = -(-units // 16) * 16
    blocks = 2 * planes
    ff = blocks * slot

    def by_group(mat):
        parts = mat.reshape(height, blocks, n, units).transpose(2, 0, 1, 3)
        return jnp.pad(parts, ((0, 0), (0, 0), (0, 0), (0, slot - units))).reshape(n, height, ff)

    gu_groups = jnp.concatenate([by_group(w_gate), by_group(w_up)], axis=-1)
    gu_parts = [
        around(lax.dynamic_index_in_dim(gu_groups, j ^ k, 0, keepdims=False), k)
        if k
        else lax.dynamic_index_in_dim(gu_groups, j, 0, keepdims=False)
        for k in range(n)
    ]
    gu_rows = jnp.concatenate(natural(gu_parts, j), axis=0)

    out_planes = jnp.stack(gather_planes(after(w_out, xs[-1])))
    gu_planes = gather_planes(after(gu_rows, xs[-1]))
    down_planes = gather_planes(after(w_down, xs[-1]))
    gu_all = [b for a in gu_planes for b in (a, swap(a))]
    down_all = [b for a in down_planes for b in (a, swap(a))]
    out_half = jnp.stack(gather_seq(out_planes))
    out_both = jnp.stack([out_half, swap(out_half)])
    out_both = jnp.stack(natural([out_both[0], out_both[1]], c))
    out_both = jnp.stack(natural([out_both[:, t] for t in range(n)], j), axis=1)
    out_both = jnp.stack(natural([out_both[:, :, t] for t in range(planes)], z), axis=0)
    out_mat = out_both.reshape(width, width)
    ogs = gather_seq(after(og, xs[-1]))

    normed, qkv_mat, qkv, lse, context = call(
        functools.partial(attend_kernel, n, docs),
        [
            out((length, width), bf16),
            out((width, 3 * group), bf16),
            out((length, 3 * group), bf16),
            out((length, HEADS // n), f32),
            out((length, group), bf16),
        ],
        [info, *xs, qkv_own, qkv_other, cosine, sine],
        flops=8 * length * width * group,
        name="attend",
    )
    contexts = gather_seq(context)
    resid, normed2, out_mine = call(
        functools.partial(project_kernel, n),
        [out((tokens, width), f32), out((length, width), bf16), out((group, width), bf16)],
        [info, *contexts, out_mat, *xs],
        scratch=[pltpu.VMEM((length, width), f32)],
        flops=2 * length * width * width,
        name="project",
    )
    block_f = out((tokens, width), f32)
    block_l = out((tokens, width), bf16)
    hidden, d_gu, dn_own, *rest = call(
        functools.partial(ffn_kernel, n, planes),
        [out((length, ff), bf16), out((length, 2 * ff), bf16), block_f]
        + [block_l] * (n - 1)
        + [out((ff, width), bf16), out((length, width), bf16)],
        [info, normed2, *gu_all, *down_all, *ogs],
        scratch=[pltpu.VMEM((width, 2 * ff), bf16), pltpu.VMEM((length, width), f32)],
        flops=10 * length * width * ff,
        name="ffn",
    )
    dn_sends = rest[: n - 1]
    down_mat, og_full = rest[n - 1 :]
    dn_parts = [dn_own] + [around(a, k + 1) for k, a in enumerate(dn_sends)]

    def grad_halves(left, right, keep_rows, name):
        m = left.shape[1]
        cols = right.shape[1]
        keep, send = call(
            grad_kernel,
            [out((planes, keep_rows, cols), f32), out((planes, keep_rows, cols), bf16)],
            [info, left, right],
            scratch=[pltpu.VMEM((m, cols), f32)],
            flops=2 * length * m * cols,
            name=name,
        )
        return keep + swap(send).astype(f32)

    gu_sum = grad_halves(normed2, d_gu, n * height, "grad_gu")
    down_sum = grad_halves(hidden, og_full, units, "grad_down")

    ho_own, *ho_sends = call(
        functools.partial(spread_kernel, n),
        [block_f] + [block_l] * (n - 1),
        [info, hidden, down_mat],
        scratch=[pltpu.VMEM((length, width), f32)],
        flops=2 * length * width * ff,
        name="hidden_out",
    )
    ho_sum = resid + ho_own
    for k, a in enumerate(ho_sends):
        ho_sum = ho_sum + around(a, k + 1).astype(f32)
    hidden_out = ho_sum.astype(bf16)

    d_resid, d_branch = call(
        functools.partial(resid_back_kernel, n),
        [block_f, block_l],
        [*dn_parts, resid, og],
        smem=0,
        name="resid_back",
    )
    branches = gather_seq(d_branch)
    d_qkv, db_full, n1_own, *n1_sends = call(
        functools.partial(attend_back_kernel, n, docs),
        [out((length, 3 * group), bf16), out((length, width), bf16), block_f] + [block_l] * (n - 1),
        [info, *branches, out_mine, qkv, lse, qkv_mat, cosine, sine],
        scratch=[pltpu.VMEM((length, group), f32)] * 3 + [pltpu.VMEM((length, width), f32)],
        flops=12 * length * width * group,
        name="attend_back",
    )
    n1_parts = [n1_own] + [around(a, k + 1) for k, a in enumerate(n1_sends)]
    qkv_sum = grad_halves(normed, d_qkv, n * height, "grad_qkv")
    (in_grad,) = call(
        functools.partial(input_back_kernel, n),
        [block_f],
        [*n1_parts, x, d_resid],
        smem=0,
        name="input_back",
    )
    keep, send = call(
        functools.partial(grad_out_kernel, n),
        [out((planes, height, width), f32), out((planes, height, width), bf16)],
        [info, *contexts, db_full],
        scratch=[
            pltpu.VMEM((width, length), f32),
            pltpu.VMEM((2 * planes * height, length), f32),
        ],
        flops=2 * length * group * width,
        name="grad_out",
    )
    out_sum = keep + swap(send).astype(f32)

    def reduce_planes(total):
        mine = lax.dynamic_index_in_dim(total, z, 0, keepdims=False)
        for k in range(1, planes):
            block = lax.dynamic_index_in_dim(total, z ^ k, 0, keepdims=False).astype(bf16)
            mine = mine + across(block, k).astype(f32)
        return mine

    grad_down = reduce_planes(down_sum)
    grad_out = reduce_planes(out_sum)

    def to_owner(total):
        cols = total.shape[-1]
        parts = to_all(total.astype(bf16).reshape(planes * n, height, cols))
        return jnp.sum(parts.reshape(planes, n, height, cols).astype(f32), axis=0)

    gu_grad = to_owner(gu_sum).reshape(n, height, 2, blocks, slot)[..., :units]
    gu_grad = gu_grad.transpose(2, 1, 3, 0, 4).reshape(2, height, blocks * n * units)
    qkv_grad = to_owner(qkv_sum).reshape(n, height, 3, group)
    qkv_grad = qkv_grad.transpose(2, 1, 0, 3).reshape(3, height, width)
    return (
        hidden_out[None],
        in_grad[None],
        qkv_grad[0],
        qkv_grad[1],
        qkv_grad[2],
        grad_out,
        gu_grad[0],
        gu_grad[1],
        grad_down,
    )


def solution(mesh):
    dp, seq = mesh.shape["dp"], mesh.shape["seq"]
    fine = Mesh(
        mesh.devices.reshape(dp // 2, 2, seq // 2, 2), ("plane", "core", "seq_hi", "seq_lo")
    )
    token = P(("plane", "core"), ("seq_hi", "seq_lo"), None)
    weight = P(("plane", "core", "seq_hi", "seq_lo"), None)
    return jax.shard_map(
        body,
        mesh=fine,
        in_specs=(token, P(("plane", "core"), None)) + (weight,) * 7 + (token,),
        out_specs=(token, token) + (weight,) * 7,
        check_vma=False,
    )
```

```python
import functools

import jax
import jax.numpy as jnp
from jax import lax
from jax.experimental import pallas as pl
from jax.experimental.pallas import tpu as pltpu
from jax.sharding import Mesh, PartitionSpec as P


HEADS = 16
HEAD_DIM = 64
eps = 1e-05
bf16 = jnp.bfloat16
f32 = jnp.float32
NN = (((1,), (0,)), ((), ()))
NT = (((1,), (1,)), ((), ()))
TN = (((0,), (0,)), ((), ()))


def dot(left, right, dims=NN):
    return lax.dot_general(left, right, dims, preferred_element_type=f32)


def rows(start, size):
    return pl.ds(pl.multiple_of(start, size), size)


def norm_parts(values):
    centred = values - jnp.mean(values, axis=-1, keepdims=True)
    inv = lax.rsqrt(jnp.mean(centred * centred, axis=-1, keepdims=True) + eps)
    return centred * inv, inv


def norm_back(normed, inv, grad):
    mean_grad = jnp.mean(grad, axis=-1, keepdims=True)
    mean_both = jnp.mean(grad * normed, axis=-1, keepdims=True)
    return (grad - mean_grad - normed * mean_both) * inv


def call(kernel, outs, args, scratch=(), flops=0, smem=1):
    vmem = pl.BlockSpec(memory_space=pltpu.VMEM)
    in_specs = [pl.BlockSpec(memory_space=pltpu.SMEM)] * smem + [vmem] * (len(args) - smem)
    moved = sum(a.size * a.dtype.itemsize for a in args) + sum(
        o.size * jnp.dtype(o.dtype).itemsize for o in outs
    )
    return pl.pallas_call(
        kernel,
        out_shape=outs,
        in_specs=in_specs,
        out_specs=[vmem] * len(outs),
        scratch_shapes=list(scratch),
        cost_estimate=pl.CostEstimate(flops=flops, bytes_accessed=moved, transcendentals=0),
        compiler_params=pltpu.CompilerParams(vmem_limit_bytes=24 * 1024 * 1024),
    )(*args)


def out(shape, dtype):
    return jax.ShapeDtypeStruct(shape, dtype)


def turn(values, cosine, sine, sign):
    width = values.shape[-1]
    half = HEAD_DIM // 2
    lane = lax.broadcasted_iota(jnp.int32, values.shape, 1)
    first = (lane & (HEAD_DIM - 1)) < half
    ahead = pltpu.roll(values, width - half, 1)
    behind = pltpu.roll(values, half, 1)
    other = jnp.where(first, -ahead, behind)
    return values * cosine + (other * sine if sign > 0 else -(other * sine))


def head_lanes(shape, head):
    lane = lax.broadcasted_iota(jnp.int32, shape, 1)
    return (lane >= head * HEAD_DIM) & (lane < (head + 1) * HEAD_DIM)


def masked(scores, starts, first_row):
    pos = lax.broadcasted_iota(jnp.int32, (scores.shape[0], 1), 0) + first_row
    begin = jnp.zeros_like(pos)
    for start in starts:
        begin = jnp.where(pos >= start, start, begin)
    keys = lax.broadcasted_iota(jnp.int32, scores.shape, 1)
    return jnp.where((keys >= begin) & (keys <= pos), scores, -1e30)


def attend_kernel(n, docs, info, *refs):
    xs = refs[:n]
    own, other, cos_ref, sin_ref = refs[n : n + 4]
    normed, mats, qkv, lse, context = refs[n + 4 :]
    j, c = info[0], info[2]
    tokens = xs[0].shape[0]
    for k in range(n):
        block, _ = norm_parts(xs[k][...].astype(f32))
        normed[rows((j ^ k) * tokens, tokens), :] = block.astype(bf16)
    planes, height = own.shape[0], own.shape[1]
    for z in range(planes):
        mats[rows((2 * z + c) * height, height), :] = own[z]
        mats[rows((2 * z + 1 - c) * height, height), :] = other[z]
    pre = dot(normed[...], mats[...])
    width = pre.shape[1] // 3
    reps = width // cos_ref.shape[1]
    cosine = jnp.concatenate([cos_ref[...]] * reps, axis=1)
    sine = jnp.concatenate([sin_ref[...]] * reps, axis=1)
    qkv[:, :width] = (
        turn(pre[:, :width], cosine, sine, 1).astype(bf16).astype(f32) * HEAD_DIM**-0.5
    ).astype(bf16)
    qkv[:, width : 2 * width] = turn(pre[:, width : 2 * width], cosine, sine, 1).astype(bf16)
    qkv[:, 2 * width :] = pre[:, 2 * width :].astype(bf16)
    starts = [info[3 + d] for d in range(docs)]
    length = qkv.shape[0]
    step = 256

    def some_rows(b, carry):
        here = rows(b * step, step)
        query = qkv[here, :width]
        total = jnp.zeros((step, width), f32)
        for head in range(width // HEAD_DIM):
            mine = head_lanes(query.shape, head)
            scores = dot(jnp.where(mine, query, 0), qkv[:, width : 2 * width], NT)
            scores = masked(scores, starts, b * step)
            top = jnp.max(scores, axis=-1, keepdims=True)
            expo = jnp.exp(scores - top)
            mass = jnp.sum(expo, axis=-1, keepdims=True)
            probs = (expo * (1.0 / mass)).astype(bf16)
            total = jnp.where(mine, dot(probs, qkv[:, 2 * width :]), total)
            lse[here, head : head + 1] = top + jnp.log(mass)
        context[here, :] = total.astype(bf16)
        return carry

    lax.fori_loop(0, length // step, some_rows, 0)


def split_in_kernel(n, *refs):
    mats, (parts,) = refs[:3], refs[3:]
    planes = parts.shape[0] // n
    width = parts.shape[2] // 3
    for group in range(n):
        for t in range(3):
            piece = mats[t][:, group * width : (group + 1) * width]
            for z in range(planes):
                parts[z * n + group, :, t * width : (t + 1) * width] = piece


def split_gu_kernel(n, units, slot, info, gate, up, *parts):
    j = info[0]
    ff = parts[0].shape[1] // 2
    for group in range(n):
        for k in range(n):

            @pl.when((j ^ k) == group)
            def unused(group=group, k=k):
                if slot > units:
                    parts[k][...] = jnp.zeros_like(parts[k])
                for t, mat in enumerate((gate, up)):
                    for b in range(ff // slot):
                        here = (b * n + group) * units
                        there = t * ff + b * slot
                        parts[k][:, there : there + units] = mat[:, here : here + units]


def join_gu_kernel(n, units, slot, info, *refs):
    parts, (gate, up) = refs[:n], refs[n:]
    j = info[0]
    ff = parts[0].shape[1] // 2
    for group in range(n):
        for k in range(n):

            @pl.when((j ^ k) == group)
            def unused(group=group, k=k):
                for t, mat in enumerate((gate, up)):
                    for b in range(ff // slot):
                        here = (b * n + group) * units
                        there = t * ff + b * slot
                        mat[:, here : here + units] = parts[k][:, there : there + units].astype(f32)


def place_kernel(info, *refs):
    parts, (whole,) = refs[:-1], refs[-1:]
    size = parts[0].shape[0]
    for k, part in enumerate(parts):
        whole[rows((info[0] ^ k) * size, size), :] = part[...]


def out_mat_kernel(n, planes, info, *refs):
    parts, (whole,) = refs[:-1], refs[-1:]
    j, z, c = info[0], info[1], info[2]
    size = parts[0].shape[1]
    for p in range(n):
        for m in range(2):
            for k in range(planes):
                at = ((2 * (z ^ k) + (c ^ m)) * n + (j ^ p)) * size
                whole[rows(at, size), :] = parts[2 * p + m][k]


def project_kernel(n, info, *refs):
    contexts = refs[:n]
    mats = refs[n]
    xs = refs[n + 1 : 2 * n + 1]
    resid_own, normed, mine, acc = refs[2 * n + 1 :]
    j = info[0]
    width = contexts[0].shape[1]
    tokens = xs[0].shape[0]
    acc[...] = dot(contexts[0][...], mats[rows(j * width, width), :])
    for p in range(1, n):
        acc[...] += dot(contexts[p][...], mats[rows((j ^ p) * width, width), :])
    mine[...] = mats[rows(j * width, width), :]
    for k in range(n):
        here = rows((j ^ k) * tokens, tokens)
        resid = xs[k][...].astype(f32) + acc[here, :]
        if k == 0:
            resid_own[...] = resid
        normed[here, :] = norm_parts(resid)[0].astype(bf16)


def ffn_kernel(n, planes, info, normed, *refs):
    gu = refs[: 2 * planes]
    down = refs[2 * planes : 4 * planes]
    grads = refs[4 * planes : 4 * planes + n]
    hidden, d_gu, own_grad, *rest = refs[4 * planes + n :]
    sends = rest[: n - 1]
    down_mat, og_full, gu_mat, acc = rest[n - 1 :]
    j, z, c = info[0], info[1], info[2]
    tokens = grads[0].shape[0]
    height = gu[0].shape[0]
    rows_in = down[0].shape[0]
    slot = down_mat.shape[0] // (2 * planes)
    if slot > rows_in:
        down_mat[...] = jnp.zeros_like(down_mat)
    for k in range(planes):
        for m in range(2):
            block = 2 * (z ^ k) + (c ^ m)
            gu_mat[rows(block * height, height), :] = gu[2 * k + m][...]
            down_mat[pl.ds(pl.multiple_of(block * slot, slot), rows_in), :] = down[2 * k + m][...]
    for k in range(n):
        og_full[rows((j ^ k) * tokens, tokens), :] = grads[k][...]
    width = hidden.shape[1]
    gate = dot(normed[...], gu_mat[:, :width])
    up = dot(normed[...], gu_mat[:, width:])
    d_hidden = dot(og_full[...], down_mat[...], NT)
    sig = 1.0 / (1.0 + jnp.exp(-gate))
    silu = gate * sig
    hidden[...] = (silu * up).astype(bf16)
    d_gu[:, :width] = (d_hidden * up * (sig + gate * sig * (1.0 - sig))).astype(bf16)
    d_gu[:, width:] = (d_hidden * silu).astype(bf16)
    acc[...] = dot(d_gu[...], gu_mat[...], NT)
    own_grad[...] = acc[rows(j * tokens, tokens), :]
    for k in range(1, n):
        sends[k - 1][...] = acc[rows((j ^ k) * tokens, tokens), :].astype(bf16)


def spread_kernel(n, info, left, right, own, *rest):
    sends = rest[: n - 1]
    acc = rest[n - 1]
    j = info[0]
    tokens = own.shape[0]
    acc[...] = dot(left[...], right[...])
    own[...] = acc[rows(j * tokens, tokens), :]
    for k in range(1, n):
        sends[k - 1][...] = acc[rows((j ^ k) * tokens, tokens), :].astype(bf16)


def resid_back_kernel(n, *refs):
    parts = refs[:n]
    resid, out_grad, d_resid, d_branch = refs[n:]
    grad = parts[0][...]
    for part in parts[1:]:
        grad = grad + part[...].astype(f32)
    normed, inv = norm_parts(resid[...])
    total = out_grad[...].astype(f32) + norm_back(normed, inv, grad)
    d_resid[...] = total
    d_branch[...] = total.astype(bf16)


def input_back_kernel(n, *refs):
    parts = refs[:n]
    x, d_resid, in_grad = refs[n:]
    grad = parts[0][...]
    for part in parts[1:]:
        grad = grad + part[...].astype(f32)
    normed, inv = norm_parts(x[...].astype(f32))
    in_grad[...] = d_resid[...] + norm_back(normed, inv, grad)


def attend_back_kernel(n, docs, info, *refs):
    branches = refs[:n]
    mine, qkv, lse, mats, cos_ref, sin_ref = refs[n : n + 6]
    d_qkv, db_full, own, *rest = refs[n + 6 :]
    sends = rest[: n - 1]
    d_key, d_value, d_query, acc = rest[n - 1 :]
    j = info[0]
    tokens = branches[0].shape[0]
    for k in range(n):
        db_full[rows((j ^ k) * tokens, tokens), :] = branches[k][...]
    length = qkv.shape[0]
    width = mine.shape[0]
    starts = [info[3 + d] for d in range(docs)]
    step = 256
    d_key[...] = jnp.zeros_like(d_key)
    d_value[...] = jnp.zeros_like(d_value)

    def some_rows(b, carry):
        here = rows(b * step, step)
        d_context = dot(db_full[here, :], mine[...], NT).astype(bf16)
        query = qkv[here, :width]
        d_q = jnp.zeros((step, width), f32)
        for head in range(width // HEAD_DIM):
            lanes = head_lanes(query.shape, head)
            q_head = jnp.where(lanes, query, 0)
            g_head = jnp.where(lanes, d_context, 0)
            keys = qkv[:, width : 2 * width]
            scores = dot(q_head, keys, NT)
            scores = masked(scores, starts, b * step)
            probs = jnp.exp(scores - lse[here, head : head + 1])
            d_probs = dot(g_head, qkv[:, 2 * width :], NT)
            delta = jnp.sum(probs * d_probs, axis=-1, keepdims=True)
            d_scores = (probs * (d_probs - delta)).astype(bf16)
            d_value[...] += dot(probs.astype(bf16), g_head, TN)
            d_key[...] += dot(d_scores, q_head, TN)
            d_q = jnp.where(lanes, dot(d_scores, keys), d_q)
        d_query[here, :] = d_q * HEAD_DIM**-0.5
        return carry

    lax.fori_loop(0, length // step, some_rows, 0)
    reps = width // cos_ref.shape[1]
    cosine = jnp.concatenate([cos_ref[...]] * reps, axis=1)
    sine = jnp.concatenate([sin_ref[...]] * reps, axis=1)
    low_q = d_query[...].astype(bf16).astype(f32)
    low_k = d_key[...].astype(bf16).astype(f32)
    d_qkv[:, :width] = turn(low_q, cosine, sine, -1).astype(bf16)
    d_qkv[:, width : 2 * width] = turn(low_k, cosine, sine, -1).astype(bf16)
    d_qkv[:, 2 * width :] = d_value[...].astype(bf16)
    acc[...] = dot(d_qkv[...], mats[...], NT)
    own[...] = acc[rows(j * tokens, tokens), :]
    for k in range(1, n):
        sends[k - 1][...] = acc[rows((j ^ k) * tokens, tokens), :].astype(bf16)


def grad_kernel(info, left, right, keep, send, acc):
    c = info[2]
    acc[...] = dot(left[...], right[...], TN)
    planes, height = keep.shape[0], keep.shape[1]
    slot = acc.shape[0] // (2 * planes)
    for z in range(planes):
        keep[z] = acc[pl.ds(pl.multiple_of((2 * z + c) * slot, slot), height), :]
        send[z] = acc[pl.ds(pl.multiple_of((2 * z + 1 - c) * slot, slot), height), :].astype(bf16)


def pick_lanes(left, picked, core, planes):
    size = left.shape[1] // (2 * planes)
    for z in range(planes):
        if size % 128:
            low = left[:, 2 * z * size : (2 * z + 1) * size]
            high = left[:, (2 * z + 1) * size : (2 * z + 2) * size]
            picked[:, z * size : (z + 1) * size] = jnp.where(core == 0, low, high)
        else:
            picked[:, z * size : (z + 1) * size] = left[:, rows((2 * z + core) * size, size)]


def grad_send_kernel(info, left, right, send, picked):
    planes, size = send.shape[0], send.shape[1]
    pick_lanes(left, picked, 1 - info[2], planes)
    product = dot(picked[...], right[...], TN)
    for z in range(planes):
        send[z] = product[z * size : (z + 1) * size].astype(bf16)


def grad_all_kernel(info, left, right, got, total, picked):
    planes, size = got.shape[0], got.shape[1]
    pick_lanes(left, picked, info[2], planes)
    product = dot(picked[...], right[...], TN)
    for z in range(planes):
        total[z] = (product[z * size : (z + 1) * size] + got[z].astype(f32)).astype(bf16)


def grad_split_kernel(info, left, right, got, own, *rest):
    sends, (picked, acc) = rest[:-2], rest[-2:]
    planes, size = got.shape[0], got.shape[1]
    z = info[1]
    pick_lanes(left, picked, info[2], planes)
    acc[...] = dot(picked[...], right[...], TN)
    own[...] = acc[rows(z * size, size), :] + got[z].astype(f32)
    for k in range(1, planes):
        block = acc[rows((z ^ k) * size, size), :] + got[z ^ k].astype(f32)
        sends[k - 1][...] = block.astype(bf16)


def add_split_kernel(info, keep, got, own, *sends):
    z = info[1]
    own[...] = keep[z] + got[z].astype(f32)
    for k in range(1, keep.shape[0]):
        sends[k - 1][...] = (keep[z ^ k] + got[z ^ k].astype(f32)).astype(bf16)


def sum_kernel(*refs):
    total = refs[0][...]
    for part in refs[1:-1]:
        total = total + part[...].astype(f32)
    refs[-1][...] = total


def sum_split_kernel(n, info, *refs):
    parts, own, sends, acc = refs[: -n - 1], refs[-n - 1], refs[-n:-1], refs[-1]
    size = own.shape[0]
    total = parts[0][...]
    for part in parts[1:]:
        total = total + part[...].astype(f32)
    acc[...] = total
    own[...] = acc[rows(info[0] * size, size), :]
    for k in range(1, n):
        sends[k - 1][...] = acc[rows((info[0] ^ k) * size, size), :].astype(bf16)


def sum_in_kernel(n, parts, *grads):
    planes = parts.shape[0] // n
    width = parts.shape[2] // 3
    for group in range(n):
        total = parts[group].astype(f32)
        for z in range(1, planes):
            total = total + parts[z * n + group].astype(f32)
        for t in range(3):
            grads[t][:, group * width : (group + 1) * width] = total[:, t * width : (t + 1) * width]


def grad_out_kernel(n, info, *refs):
    contexts = refs[:n]
    right, keep, send, turned, left = refs[n:]
    j, c = info[0], info[2]
    width = contexts[0].shape[1]
    for p in range(n):
        turned[rows((j ^ p) * width, width), :] = contexts[p][...].astype(f32).T
    planes, height = keep.shape[0], keep.shape[1]
    block = height * n
    for m in range(2):
        for z in range(planes):
            at = (2 * z + (c ^ m)) * block + j * height
            left[pl.ds((m * planes + z) * height, height), :] = turned[
                pl.ds(pl.multiple_of(at, height), height), :
            ]
    product = dot(left[...].astype(bf16), right[...])
    for z in range(planes):
        keep[z] = product[z * height : (z + 1) * height]
        send[z] = product[(planes + z) * height : (planes + z + 1) * height].astype(bf16)


def layer(hidden_in, doc_starts, w_query, w_key, w_value, w_out, w_gate, w_up, w_down, out_grad):
    x = hidden_in[0]
    og = out_grad[0]
    tokens, width = x.shape
    seq = ("seq_hi", "seq_lo")
    n = lax.axis_size(seq)
    planes = lax.axis_size("plane")
    length = tokens * n
    group = HEADS // n * HEAD_DIM
    docs = doc_starts.shape[1]
    height = w_query.shape[0]
    strip = n * height
    units = w_down.shape[0]
    slot = -(-units // 16) * 16
    ff = 2 * planes * slot
    j = lax.axis_index(seq)
    z = lax.axis_index("plane")
    c = lax.axis_index("core")
    info = jnp.concatenate([jnp.stack([j, z, c]).astype(jnp.int32), doc_starts[0]])

    def swap(a):
        return lax.ppermute(a, "core", [(0, 1), (1, 0)])

    def around(a, k):
        return lax.ppermute(a, seq, [(t, t ^ k) for t in range(n)])

    def across(a, k):
        return lax.ppermute(a, "plane", [(t, t ^ k) for t in range(planes)])

    def gather_seq(a):
        return [a] + [around(a, k) for k in range(1, n)]

    def gather_planes(a):
        return [a] + [across(a, k) for k in range(1, planes)]

    def send_seq(own, sends):
        return [own] + [around(a, k + 1) for k, a in enumerate(sends)]

    def send_planes(own, sends):
        return [own] + [across(a, k + 1) for k, a in enumerate(sends)]

    def to_all(blocks):
        axes = ("plane",) + seq
        return lax.all_to_all(blocks, axes, split_axis=0, concat_axis=0, tiled=True)

    def run(kernel, outs, args, **kw):
        return call(kernel, outs, args, **kw)

    half = HEAD_DIM // 2
    freq = 10000.0 ** (-(jnp.arange(half, dtype=f32) * 2.0) / HEAD_DIM)
    lane_freq = jnp.concatenate([freq] * (128 // half))
    angle = jnp.arange(length, dtype=f32)[:, None] * lane_freq[None, :]
    cosine, sine = jnp.cos(angle), jnp.sin(angle)

    (in_parts,) = run(
        functools.partial(split_in_kernel, n),
        [out((planes * n, height, 3 * group), bf16)],
        [w_query, w_key, w_value],
        smem=0,
    )
    qkv_own = to_all(in_parts).reshape(planes, strip, 3 * group)
    qkv_other = swap(qkv_own)
    xs = gather_seq(x)

    gu_parts = run(
        functools.partial(split_gu_kernel, n, units, slot),
        [out((height, 2 * ff), bf16)] * n,
        [info, w_gate, w_up],
    )
    (gu_rows,) = run(
        place_kernel, [out((strip, 2 * ff), bf16)], [info, *send_seq(gu_parts[0], gu_parts[1:])]
    )
    gu_all = [b for a in gather_planes(gu_rows) for b in (a, swap(a))]
    down_all = [b for a in gather_planes(w_down) for b in (a, swap(a))]
    out_planes = jnp.stack(gather_planes(w_out))
    out_parts = [b for a in gather_seq(out_planes) for b in (a, swap(a))]
    (out_mat,) = run(
        functools.partial(out_mat_kernel, n, planes),
        [out((width, width), bf16)],
        [info, *out_parts],
    )
    ogs = gather_seq(og)

    normed, qkv_mat, qkv, lse, context = run(
        functools.partial(attend_kernel, n, docs),
        [
            out((length, width), bf16),
            out((width, 3 * group), bf16),
            out((length, 3 * group), bf16),
            out((length, HEADS // n), f32),
            out((length, group), bf16),
        ],
        [info, *xs, qkv_own, qkv_other, cosine, sine],
        flops=8 * length * width * group,
    )
    contexts = gather_seq(context)
    resid, normed2, out_mine = run(
        functools.partial(project_kernel, n),
        [out((tokens, width), f32), out((length, width), bf16), out((group, width), bf16)],
        [info, *contexts, out_mat, *xs],
        scratch=[pltpu.VMEM((length, width), f32)],
        flops=2 * length * width * width,
    )
    block_f = out((tokens, width), f32)
    block_l = out((tokens, width), bf16)
    hidden, d_gu, dn_own, *rest = run(
        functools.partial(ffn_kernel, n, planes),
        [out((length, ff), bf16), out((length, 2 * ff), bf16), block_f]
        + [block_l] * (n - 1)
        + [out((ff, width), bf16), out((length, width), bf16)],
        [info, normed2, *gu_all, *down_all, *ogs],
        scratch=[pltpu.VMEM((width, 2 * ff), bf16), pltpu.VMEM((length, width), f32)],
        flops=10 * length * width * ff,
    )
    down_mat, og_full = rest[n - 1 :]
    dn_parts = send_seq(dn_own, rest[: n - 1])

    def grad_halves(left, right, last, outs, scratch):
        cols = right.shape[1]
        size = left.shape[1] // (2 * planes)
        picked = pltpu.VMEM((length, size * planes), bf16)
        flops = length * left.shape[1] * cols
        (send,) = run(
            grad_send_kernel,
            [out((planes, size, cols), bf16)],
            [info, left, right],
            scratch=[picked],
            flops=flops,
        )
        got = swap(send)
        return run(last[1], outs, [info, left, right, got], scratch=[picked] + scratch, flops=flops)

    cols = 2 * ff
    own, *sends = grad_halves(
        normed2,
        d_gu,
        ("_split", grad_split_kernel),
        [out((strip, cols), f32)] + [out((strip, cols), bf16)] * (planes - 1),
        [pltpu.VMEM((strip * planes, cols), f32)],
    )
    own, *sends = run(
        functools.partial(sum_split_kernel, n),
        [out((height, cols), f32)] + [out((height, cols), bf16)] * (n - 1),
        [info, *send_planes(own, sends)],
        scratch=[pltpu.VMEM((strip, cols), f32)],
    )
    grad_gate, grad_up = run(
        functools.partial(join_gu_kernel, n, units, slot),
        [out(w_gate.shape, f32)] * 2,
        [info, *send_seq(own, sends)],
    )

    def reduce_planes(keep, send):
        size, cols = keep.shape[1:]
        own, *sends = run(
            add_split_kernel,
            [out((size, cols), f32)] + [out((size, cols), bf16)] * (planes - 1),
            [info, keep, swap(send)],
        )
        parts = send_planes(own, sends)
        (total,) = run(sum_kernel, [out((size, cols), f32)], parts, smem=0)
        return total

    keep, send = run(
        grad_kernel,
        [out((planes, units, width), f32), out((planes, units, width), bf16)],
        [info, hidden, og_full],
        scratch=[pltpu.VMEM((ff, width), f32)],
        flops=2 * length * ff * width,
    )
    grad_down = reduce_planes(keep, send)

    ho_own, *sends = run(
        functools.partial(spread_kernel, n),
        [block_f] + [block_l] * (n - 1),
        [info, hidden, down_mat],
        scratch=[pltpu.VMEM((length, width), f32)],
        flops=2 * length * width * ff,
    )
    ho_sum = resid
    for a in send_seq(ho_own, sends):
        ho_sum = ho_sum + a.astype(f32)
    hidden_out = ho_sum.astype(bf16)

    d_resid, d_branch = run(
        functools.partial(resid_back_kernel, n), [block_f, block_l], [*dn_parts, resid, og], smem=0
    )
    branches = gather_seq(d_branch)
    d_qkv, db_full, n1_own, *sends = run(
        functools.partial(attend_back_kernel, n, docs),
        [out((length, 3 * group), bf16), out((length, width), bf16), block_f] + [block_l] * (n - 1),
        [info, *branches, out_mine, qkv, lse, qkv_mat, cosine, sine],
        scratch=[pltpu.VMEM((length, group), f32)] * 3 + [pltpu.VMEM((length, width), f32)],
        flops=12 * length * width * group,
    )
    n1_parts = send_seq(n1_own, sends)
    (in_grad,) = run(
        functools.partial(input_back_kernel, n), [block_f], [*n1_parts, x, d_resid], smem=0
    )
    (in_sum,) = grad_halves(
        normed, d_qkv, ("_all", grad_all_kernel), [out((planes, strip, 3 * group), bf16)], []
    )
    in_sum = to_all(in_sum.reshape(planes * n, height, 3 * group))
    in_grads = run(
        functools.partial(sum_in_kernel, n), [out(w_query.shape, f32)] * 3, [in_sum], smem=0
    )
    keep, send = run(
        functools.partial(grad_out_kernel, n),
        [out((planes, height, width), f32), out((planes, height, width), bf16)],
        [info, *contexts, db_full],
        scratch=[
            pltpu.VMEM((width, length), f32),
            pltpu.VMEM((2 * planes * height, length), f32),
        ],
        flops=2 * length * group * width,
    )
    grad_out = reduce_planes(keep, send)
    return (
        hidden_out[None], in_grad[None], *in_grads, grad_out, grad_gate, grad_up, grad_down
    )


def solution(mesh):
    dp, seq = mesh.shape["dp"], mesh.shape["seq"]
    fine = Mesh(
        mesh.devices.reshape(dp // 2, 2, seq // 2, 2), ("plane", "core", "seq_hi", "seq_lo")
    )
    token = P(("plane", "core"), ("seq_hi", "seq_lo"), None)
    weight = P(("plane", "core", "seq_hi", "seq_lo"), None)
    return jax.shard_map(
        layer,
        mesh=fine,
        in_specs=(token, P(("plane", "core"), None)) + (weight,) * 7 + (token,),
        out_specs=(token, token) + (weight,) * 7,
        check_vma=False,
    )
```

```python
import functools
import typing

import jax
import jax.numpy as jnp
from jax import lax
from jax.experimental import pallas as pl
from jax.experimental.pallas import tpu as pltpu
from jax.sharding import Mesh, PartitionSpec as P


HEADS = 16
HEAD_DIM = 64
eps = 1e-05
bf16 = jnp.bfloat16
f32 = jnp.float32
NN = (((1,), (0,)), ((), ()))
NT = (((1,), (1,)), ((), ()))
TN = (((0,), (0,)), ((), ()))


def dot(left, right, dims=NN):
    return lax.dot_general(left, right, dims, preferred_element_type=f32)


def rows(start, size):
    return pl.ds(pl.multiple_of(start, size), size)


def norm_parts(values):
    centred = values - jnp.mean(values, axis=-1, keepdims=True)
    inv = lax.rsqrt(jnp.mean(centred * centred, axis=-1, keepdims=True) + eps)
    return centred * inv, inv


def norm_back(normed, inv, grad):
    mean_grad = jnp.mean(grad, axis=-1, keepdims=True)
    mean_both = jnp.mean(grad * normed, axis=-1, keepdims=True)
    return (grad - mean_grad - normed * mean_both) * inv


def call(kernel, outs, args, scratch=(), flops=0, smem=1, limit=24):
    vmem = pl.BlockSpec(memory_space=pltpu.VMEM)
    in_specs = [pl.BlockSpec(memory_space=pltpu.SMEM)] * smem + [vmem] * (len(args) - smem)
    moved = sum(a.size * a.dtype.itemsize for a in args) + sum(
        o.size * jnp.dtype(o.dtype).itemsize for o in outs
    )
    return pl.pallas_call(
        kernel,
        out_shape=outs,
        in_specs=in_specs,
        out_specs=[vmem] * len(outs),
        scratch_shapes=list(scratch),
        cost_estimate=pl.CostEstimate(flops=flops, bytes_accessed=moved, transcendentals=0),
        compiler_params=pltpu.CompilerParams(vmem_limit_bytes=limit * 1024 * 1024),
    )(*args)


def out(shape, dtype):
    return jax.ShapeDtypeStruct(shape, dtype)


def turn(values, cosine, sine, sign):
    width = values.shape[-1]
    half = HEAD_DIM // 2
    lane = lax.broadcasted_iota(jnp.int32, values.shape, 1)
    first = (lane & (HEAD_DIM - 1)) < half
    ahead = pltpu.roll(values, width - half, 1)
    behind = pltpu.roll(values, half, 1)
    other = jnp.where(first, -ahead, behind)
    return values * cosine + (other * sine if sign > 0 else -(other * sine))


def head_lanes(shape, head):
    lane = lax.broadcasted_iota(jnp.int32, shape, 1)
    return (lane >= head * HEAD_DIM) & (lane < (head + 1) * HEAD_DIM)


def masked(scores, starts, first_row):
    pos = lax.broadcasted_iota(jnp.int32, (scores.shape[0], 1), 0) + first_row
    begin = jnp.zeros_like(pos)
    for start in starts:
        begin = jnp.where(pos >= start, start, begin)
    keys = lax.broadcasted_iota(jnp.int32, scores.shape, 1)
    return jnp.where((keys >= begin) & (keys <= pos), scores, -1e30)


def attend_kernel(d, docs, info, *refs):
    n = d.n
    count = 2 * sum(ways(d.planes))
    xs, blocks = refs[:n], refs[n : n + count]
    cos_ref, sin_ref, normed, mats, qkv, lse, context = refs[n + count :]
    j = info[0]
    tokens = xs[0].shape[0]
    for k in range(n):
        block, _ = norm_parts(xs[k][...].astype(f32))
        normed[rows((j ^ k) * tokens, tokens), :] = block.astype(bf16)

    def put(block, source):
        here = rows(block * d.strip, d.strip)
        for t in range(d.in_tiles):
            mats[here, t * 128 : (t + 1) * 128] = source[t * d.strip : (t + 1) * d.strip, :]

    each_block(d, info, blocks, put)
    pre = dot(normed[...], mats[...])
    width = pre.shape[1] // 3
    reps = width // cos_ref.shape[1]
    cosine = jnp.concatenate([cos_ref[...]] * reps, axis=1)
    sine = jnp.concatenate([sin_ref[...]] * reps, axis=1)
    qkv[:, :width] = (
        turn(pre[:, :width], cosine, sine, 1).astype(bf16).astype(f32) * HEAD_DIM**-0.5
    ).astype(bf16)
    qkv[:, width : 2 * width] = turn(pre[:, width : 2 * width], cosine, sine, 1).astype(bf16)
    qkv[:, 2 * width :] = pre[:, 2 * width :].astype(bf16)
    starts = [info[3 + d] for d in range(docs)]
    length = qkv.shape[0]
    step = 256

    def some_rows(b, carry):
        here = rows(b * step, step)
        query = qkv[here, :width]
        total = jnp.zeros((step, width), f32)
        for head in range(width // HEAD_DIM):
            mine = head_lanes(query.shape, head)
            scores = dot(jnp.where(mine, query, 0), qkv[:, width : 2 * width], NT)
            scores = masked(scores, starts, b * step)
            top = jnp.max(scores, axis=-1, keepdims=True)
            expo = jnp.exp(scores - top)
            mass = jnp.sum(expo, axis=-1, keepdims=True)
            probs = (expo * (1.0 / mass)).astype(bf16)
            total = jnp.where(mine, dot(probs, qkv[:, 2 * width :]), total)
            lse[here, head : head + 1] = top + jnp.log(mass)
        context[here, :] = total.astype(bf16)
        return carry

    lax.fori_loop(0, length // step, some_rows, 0)


class Dims(typing.NamedTuple):
    n: int
    planes: int
    height: int
    units: int
    slot: int
    width: int
    group: int

    @property
    def strip(self):
        return self.n * self.height

    @property
    def ff(self):
        return 2 * self.planes * self.slot

    @property
    def whole(self):
        return self.ff // 128 if self.shared else -(-self.ff // 128)

    @property
    def shared(self):
        return self.ff % 128 == 64

    @property
    def tiles(self):
        return 2 * self.whole + self.shared

    @property
    def wide(self):
        return (self.whole + self.shared) * 128

    @property
    def gu_rows(self):
        return self.tiles * self.strip

    @property
    def in_tiles(self):
        return 3 * self.group // 128

    @property
    def payload(self):
        return self.gu_rows + self.width // 128 * self.slot


def ways(planes):
    return (1, 1, 2, 2) if planes == 4 else (1,) * planes


def each_block(d, info, refs, place):
    z, c = info[1], info[2]
    outer = (z == 0) | (z == d.planes - 1)
    at = 0
    for k, count in enumerate(ways(d.planes)):
        for a in range(count):
            for m in range(2):
                put = functools.partial(place, 2 * (z ^ k) + (c ^ m), refs[at])
                at += 1
                if count == 1:
                    put()
                else:
                    pl.when(outer if a == 0 else jnp.logical_not(outer))(put)


def gate_up_tile(d, gate, up, t):
    if t < d.whole:
        return gate[:, t * 128 : (t + 1) * 128]
    if t < 2 * d.whole:
        return up[:, (t - d.whole) * 128 : (t - d.whole + 1) * 128]
    at = d.whole * 128
    return jnp.concatenate([gate[:, at : at + 64], up[:, at : at + 64]], axis=1)


def pack_kernel(first, second, whole):
    whole[: first.shape[0], :] = first[...]
    whole[first.shape[0] :, :] = second[...]


def split_kernel(d, info, *refs):
    mats, (w_gate, w_up), pieces = refs[:3], refs[3:5], refs[5 : 5 + d.n]
    gate, up = refs[5 + d.n :]
    if d.slot > d.units:
        gate[...] = jnp.zeros_like(gate)
        up[...] = jnp.zeros_like(up)
    for group in range(d.n):
        for b in range(2 * d.planes):
            here = (b * d.n + group) * d.units
            there = slice(b * d.slot, b * d.slot + d.units)
            gate[:, there] = w_gate[:, here : here + d.units]
            up[:, there] = w_up[:, here : here + d.units]
        for k in range(d.n):

            @pl.when((info[0] ^ k) == group)
            def unused(group=group, k=k):
                for t in range(d.tiles):
                    tile = gate_up_tile(d, gate, up, t)
                    pieces[k][t * d.height : (t + 1) * d.height, :] = tile
                for t in range(d.in_tiles):
                    at = d.tiles + t
                    which, lane = divmod(t * 128, d.group)
                    lane += group * d.group
                    pieces[k][at * d.height : (at + 1) * d.height, :] = mats[which][
                        :, lane : lane + 128
                    ]


def place_kernel(d, info, *refs):
    pieces, (in_payload, gu_payload) = refs[: d.n], refs[d.n :]
    for k in range(d.n):
        for t in range(d.tiles + d.in_tiles):
            inner = t >= d.tiles
            at = (t - d.tiles if inner else t) * d.strip + (info[0] ^ k) * d.height
            piece = pieces[k][t * d.height : (t + 1) * d.height, :]
            (in_payload if inner else gu_payload)[rows(at, d.height), :] = piece


def join_kernel(d, info, *refs):
    pieces, (grad_gate, grad_up, gate, up) = refs[: d.n], refs[d.n :]
    for group in range(d.n):
        for k in range(d.n):

            @pl.when((info[0] ^ k) == group)
            def unused(k=k):
                for t in range(d.tiles):
                    tile = pieces[k][t * d.height : (t + 1) * d.height, :].astype(f32)
                    if t < d.whole:
                        gate[:, t * 128 : (t + 1) * 128] = tile
                    elif t < 2 * d.whole:
                        up[:, (t - d.whole) * 128 : (t - d.whole + 1) * 128] = tile
                    else:
                        gate[:, d.whole * 128 : d.whole * 128 + 64] = tile[:, :64]
                        up[:, d.whole * 128 : d.whole * 128 + 64] = tile[:, 64:]

        for b in range(2 * d.planes):
            there = (b * d.n + group) * d.units
            here = slice(b * d.slot, b * d.slot + d.units)
            grad_gate[:, there : there + d.units] = gate[:, here]
            grad_up[:, there : there + d.units] = up[:, here]


def out_mat_kernel(n, planes, info, *refs):
    parts, (whole,) = refs[:-1], refs[-1:]
    j, z, c = info[0], info[1], info[2]
    size = parts[0].shape[1]
    for p in range(n):
        for m in range(2):
            for k in range(planes):
                at = ((2 * (z ^ k) + (c ^ m)) * n + (j ^ p)) * size
                whole[rows(at, size), :] = parts[2 * p + m][k]


def project_kernel(n, info, *refs):
    contexts = refs[:n]
    mats = refs[n]
    xs = refs[n + 1 : 2 * n + 1]
    resid_own, normed, acc = refs[2 * n + 1 :]
    j = info[0]
    width = contexts[0].shape[1]
    tokens = xs[0].shape[0]
    acc[...] = dot(contexts[0][...], mats[rows(j * width, width), :])
    for p in range(1, n):
        acc[...] += dot(contexts[p][...], mats[rows((j ^ p) * width, width), :])
    for k in range(n):
        here = rows((j ^ k) * tokens, tokens)
        resid = xs[k][...].astype(f32) + acc[here, :]
        if k == 0:
            resid_own[...] = resid
        normed[here, :] = norm_parts(resid)[0].astype(bf16)


def gate_part(d, both):
    if d.shared:
        at = 2 * d.whole * 128
        return jnp.concatenate([both[:, : d.whole * 128], both[:, at:]], axis=1)
    return both[:, : d.whole * 128]


def up_part(d, both):
    at = d.whole * 128
    if d.shared:
        last = pltpu.roll(both[:, 2 * at :], 64, 1)
        return jnp.concatenate([both[:, at : 2 * at], last], axis=1)
    return both[:, at:]


def ffn_kernel(d, info, normed, *refs):
    count = 2 * sum(ways(d.planes))
    blocks, downs = refs[:count], refs[count : 2 * count]
    grads = refs[2 * count : 2 * count + d.n]
    hidden, d_gu, own_grad, *rest = refs[2 * count + d.n :]
    sends = rest[: d.n - 1]
    down_mat, og_full, gu_mat, acc = rest[d.n - 1 :]
    j = info[0]
    tokens = grads[0].shape[0]
    if d.slot > d.units:
        down_mat[...] = jnp.zeros_like(down_mat)
    elif d.wide > d.ff:
        down_mat[d.ff :, :] = jnp.zeros((d.wide - d.ff, d.width), bf16)

    def put_gu(block, source):
        here = rows(block * d.strip, d.strip)
        for t in range(d.tiles):
            gu_mat[here, t * 128 : (t + 1) * 128] = source[t * d.strip : (t + 1) * d.strip, :]

    def put_down(block, source):
        at = pl.multiple_of(block * d.slot, d.slot)
        down_mat[pl.ds(at, d.units), :] = source[d.height :, :]

    each_block(d, info, blocks, put_gu)
    each_block(d, info, downs, put_down)
    for k in range(d.n):
        og_full[rows((j ^ k) * tokens, tokens), :] = grads[k][...]
    both = dot(normed[...], gu_mat[...])
    d_hidden = dot(og_full[...], down_mat[...], NT)
    gate, up = gate_part(d, both), up_part(d, both)
    sig = 1.0 / (1.0 + jnp.exp(-gate))
    silu = gate * sig
    mixed = silu * up
    d_gate = d_hidden * up * (sig + gate * sig * (1.0 - sig))
    d_up = d_hidden * silu
    at = d.whole * 128
    if d.shared:
        lane = lax.broadcasted_iota(jnp.int32, (mixed.shape[0], 128), 1)
        hidden[:, :at] = mixed[:, :at].astype(bf16)
        hidden[:, at:] = jnp.where(lane < 64, mixed[:, at:], 0.0).astype(bf16)
        last = jnp.where(lane < 64, d_gate[:, at:], pltpu.roll(d_up[:, at:], 64, 1))
        d_gu[:, 2 * at :] = last.astype(bf16)
    else:
        hidden[...] = mixed.astype(bf16)
    d_gu[:, :at] = d_gate[:, :at].astype(bf16)
    d_gu[:, at : 2 * at] = d_up[:, :at].astype(bf16)
    acc[...] = dot(d_gu[...], gu_mat[...], NT)
    own_grad[...] = acc[rows(j * tokens, tokens), :]
    for k in range(1, d.n):
        sends[k - 1][...] = acc[rows((j ^ k) * tokens, tokens), :].astype(bf16)


def hidden_out_kernel(n, info, left, right, branch, own, *rest):
    sends, acc = rest[:-1], rest[-1]
    j = info[0]
    tokens = own.shape[0]
    acc[...] = dot(left[...], right[...])
    own[...] = acc[rows(j * tokens, tokens), :]
    for k in range(1, n):
        sends[k - 1][:tokens, :] = acc[rows((j ^ k) * tokens, tokens), :].astype(bf16)
        sends[k - 1][tokens:, :] = branch[...]


def hidden_sum_kernel(resid, own, *refs):
    total = resid[...] + own[...]
    for part in refs[:-1]:
        total = total + part[: own.shape[0], :].astype(f32)
    refs[-1][...] = total.astype(bf16)


def resid_back_kernel(n, info, *refs):
    parts = refs[:n]
    resid, out_grad, mats, d_resid, d_branch, *pieces, acc = refs[n:]
    grad = parts[0][...]
    for part in parts[1:]:
        grad = grad + part[...].astype(f32)
    normed, inv = norm_parts(resid[...])
    total = out_grad[...].astype(f32) + norm_back(normed, inv, grad)
    d_resid[...] = total
    d_branch[...] = total.astype(bf16)
    acc[...] = dot(total.astype(bf16), mats[...], NT)
    width = pieces[0].shape[1]
    for k in range(n):
        pieces[k][...] = acc[:, rows((info[0] ^ k) * width, width)].astype(bf16)


def input_back_kernel(n, *refs):
    parts = refs[:n]
    x, d_resid, in_grad = refs[n:]
    grad = parts[0][...]
    for part in parts[1:]:
        grad = grad + part[...].astype(f32)
    normed, inv = norm_parts(x[...].astype(f32))
    in_grad[...] = d_resid[...] + norm_back(normed, inv, grad)


def attend_back_kernel(n, docs, info, *refs):
    pieces = refs[:n]
    qkv, lse, mats, cos_ref, sin_ref = refs[n : n + 5]
    d_qkv, own, *rest = refs[n + 5 :]
    sends = rest[: n - 1]
    d_key, d_value, d_query, d_contexts, acc = rest[n - 1 :]
    j = info[0]
    tokens, width = pieces[0].shape
    for k in range(n):
        d_contexts[rows((j ^ k) * tokens, tokens), :] = pieces[k][...]
    length = qkv.shape[0]
    starts = [info[3 + d] for d in range(docs)]
    step = 256
    d_key[...] = jnp.zeros_like(d_key)
    d_value[...] = jnp.zeros_like(d_value)

    def some_rows(b, carry):
        here = rows(b * step, step)
        d_context = d_contexts[here, :]
        query = qkv[here, :width]
        d_q = jnp.zeros((step, width), f32)
        for head in range(width // HEAD_DIM):
            lanes = head_lanes(query.shape, head)
            q_head = jnp.where(lanes, query, 0)
            g_head = jnp.where(lanes, d_context, 0)
            keys = qkv[:, width : 2 * width]
            scores = dot(q_head, keys, NT)
            scores = masked(scores, starts, b * step)
            probs = jnp.exp(scores - lse[here, head : head + 1])
            d_probs = dot(g_head, qkv[:, 2 * width :], NT)
            delta = jnp.sum(probs * d_probs, axis=-1, keepdims=True)
            d_scores = (probs * (d_probs - delta)).astype(bf16)
            d_value[...] += dot(probs.astype(bf16), g_head, TN)
            d_key[...] += dot(d_scores, q_head, TN)
            d_q = jnp.where(lanes, dot(d_scores, keys), d_q)
        d_query[here, :] = d_q * HEAD_DIM**-0.5
        return carry

    lax.fori_loop(0, length // step, some_rows, 0)
    reps = width // cos_ref.shape[1]
    cosine = jnp.concatenate([cos_ref[...]] * reps, axis=1)
    sine = jnp.concatenate([sin_ref[...]] * reps, axis=1)
    low_q = d_query[...].astype(bf16).astype(f32)
    low_k = d_key[...].astype(bf16).astype(f32)
    d_qkv[:, :width] = turn(low_q, cosine, sine, -1).astype(bf16)
    d_qkv[:, width : 2 * width] = turn(low_k, cosine, sine, -1).astype(bf16)
    d_qkv[:, 2 * width :] = d_value[...].astype(bf16)
    acc[...] = dot(d_qkv[...], mats[...], NT)
    own[...] = acc[rows(j * tokens, tokens), :]
    for k in range(1, n):
        sends[k - 1][...] = acc[rows((j ^ k) * tokens, tokens), :].astype(bf16)


def pick_lanes(left, picked, core, planes):
    size = left.shape[1] // (2 * planes)
    for z in range(planes):
        if size % 128:
            low = left[:, 2 * z * size : (2 * z + 1) * size]
            high = left[:, (2 * z + 1) * size : (2 * z + 2) * size]
            picked[:, z * size : (z + 1) * size] = jnp.where(core == 0, low, high)
        else:
            picked[:, z * size : (z + 1) * size] = left[:, rows((2 * z + core) * size, size)]


def grad_send_kernel(info, left, right, send, picked):
    planes, size = send.shape[0], send.shape[1]
    pick_lanes(left, picked, 1 - info[2], planes)
    product = dot(picked[...], right[...], TN)
    for z in range(planes):
        send[z] = product[z * size : (z + 1) * size].astype(bf16)


def grad_all_kernel(info, left, right, got, total, picked):
    planes, size = got.shape[0], got.shape[1]
    pick_lanes(left, picked, info[2], planes)
    product = dot(picked[...], right[...], TN)
    for z in range(planes):
        total[z] = (product[z * size : (z + 1) * size] + got[z].astype(f32)).astype(bf16)


def ffn_send_kernel(d, info, normed, d_gu, hidden, og_full, keep, send, picked, acc):
    c = info[2]
    pick_lanes(normed, picked, 1 - c, d.planes)
    product = dot(picked[...], d_gu[...], TN).astype(bf16)
    acc[...] = dot(hidden[...], og_full[...], TN)
    for z in range(d.planes):
        for t in range(d.tiles):
            send[z, t * d.strip : (t + 1) * d.strip, :] = product[
                z * d.strip : (z + 1) * d.strip, t * 128 : (t + 1) * 128
            ]
        keep[z] = acc[rows((2 * z + c) * d.slot, d.slot), :]
        other = acc[rows((2 * z + 1 - c) * d.slot, d.slot), :].astype(bf16)
        for t in range(d.width // 128):
            at = d.gu_rows + t * d.slot
            send[z, at : at + d.slot, :] = other[:, t * 128 : (t + 1) * 128]


def ffn_split_kernel(d, info, normed, d_gu, keep, got, own_gu, own_down, *rest):
    sends, (picked, acc) = rest[:-2], rest[-2:]
    z = info[1]
    pick_lanes(normed, picked, info[2], d.planes)
    acc[...] = dot(picked[...], d_gu[...], TN)
    for k in range(d.planes):
        for t in range(d.tiles):
            here = slice(t * d.strip, (t + 1) * d.strip)
            lanes = slice(t * 128, (t + 1) * 128)
            total = acc[rows((z ^ k) * d.strip, d.strip), lanes] + got[z ^ k, here, :].astype(f32)
            if k:
                sends[k - 1][here, :] = total.astype(bf16)
            else:
                own_gu[:, lanes] = total
        for t in range(d.width // 128):
            here = slice(d.gu_rows + t * d.slot, d.gu_rows + (t + 1) * d.slot)
            lanes = slice(t * 128, (t + 1) * 128)
            total = keep[z ^ k, :, lanes] + got[z ^ k, here, :].astype(f32)
            if k:
                sends[k - 1][here, :] = total.astype(bf16)
            else:
                own_down[:, lanes] = total


def ffn_mid_kernel(info, near, far, *refs):
    (first, second, third), (to_pair, to_mid) = refs[:3], refs[3:]
    inner = (info[1] == 1) | (info[1] == 2)
    passed = jnp.where(inner, second[...].astype(f32) + third[...].astype(f32), 0.0)
    to_pair[...] = (near[...].astype(f32) + passed).astype(bf16)
    to_mid[...] = (far[...].astype(f32) + first[...].astype(f32)).astype(bf16)


def ffn_sum_kernel(d, info, own_gu, own_down, *refs):
    count = 2 if d.planes == 4 else d.planes - 1
    parts = refs[:count]
    grad_down, *pieces, acc = refs[count:]
    inner = (info[1] == 1) | (info[1] == 2)

    def add(total, here):
        for k, part in enumerate(parts):
            block = part[here, :].astype(f32)
            total = total + (jnp.where(inner, block, 0.0) if k and d.planes == 4 else block)
        return total

    for t in range(d.tiles):
        acc[...] = add(own_gu[:, t * 128 : (t + 1) * 128], slice(t * d.strip, (t + 1) * d.strip))
        for k in range(d.n):
            pieces[k][t * d.height : (t + 1) * d.height, :] = acc[
                rows((info[0] ^ k) * d.height, d.height), :
            ].astype(bf16)
    for t in range(d.width // 128):
        at, lanes = d.gu_rows + t * d.slot, slice(t * 128, (t + 1) * 128)
        grad_down[:, lanes] = add(own_down[: d.units, lanes], slice(at, at + d.units))


def add_split_kernel(info, keep, got, own, *sends):
    z = info[1]
    own[...] = keep[z] + got[z].astype(f32)
    for k in range(1, keep.shape[0]):
        sends[k - 1][...] = (keep[z ^ k] + got[z ^ k].astype(f32)).astype(bf16)


def sum_kernel(*refs):
    total = refs[0][...]
    for part in refs[1:-1]:
        total = total + part[...].astype(f32)
    refs[-1][...] = total


def sum_in_kernel(n, parts, *grads):
    planes = parts.shape[0] // n
    width = parts.shape[2] // 3
    for group in range(n):
        total = parts[group].astype(f32)
        for z in range(1, planes):
            total = total + parts[z * n + group].astype(f32)
        for t in range(3):
            grads[t][:, group * width : (group + 1) * width] = total[:, t * width : (t + 1) * width]


def grad_out_kernel(n, info, *refs):
    contexts, branches = refs[:n], refs[n : 2 * n]
    keep, send, turned, left, right = refs[2 * n :]
    j, c = info[0], info[2]
    width = contexts[0].shape[1]
    tokens = branches[0].shape[0]
    for p in range(n):
        block = branches[p][tokens:, :] if p else branches[p][...]
        right[rows((j ^ p) * tokens, tokens), :] = block
        turned[rows((j ^ p) * width, width), :] = contexts[p][...].astype(f32).T
    planes, height = keep.shape[0], keep.shape[1]
    block = height * n
    for m in range(2):
        for z in range(planes):
            at = (2 * z + (c ^ m)) * block + j * height
            left[pl.ds((m * planes + z) * height, height), :] = turned[
                pl.ds(pl.multiple_of(at, height), height), :
            ]
    product = dot(left[...].astype(bf16), right[...])
    for z in range(planes):
        keep[z] = product[z * height : (z + 1) * height]
        send[z] = product[(planes + z) * height : (planes + z + 1) * height].astype(bf16)


MIDDLE = ((2, 4), (3, 5), (4, 2), (5, 3), (0, 1), (1, 0), (6, 7), (7, 6))
LAST = tuple((2 * a + t, 2 * b + t) for a, b in ((1, 3), (2, 0), (0, 1), (3, 2)) for t in range(2))
FIRST = tuple((b, a) for a, b in LAST)


def layer(hidden_in, doc_starts, w_query, w_key, w_value, w_out, w_gate, w_up, w_down, out_grad):
    x = hidden_in[0]
    og = out_grad[0]
    tokens, width = x.shape
    seq = ("seq_hi", "seq_lo")
    n = lax.axis_size(seq)
    planes = lax.axis_size("plane")
    length = tokens * n
    group = HEADS // n * HEAD_DIM
    docs = doc_starts.shape[1]
    height = w_query.shape[0]
    strip = n * height
    units = w_down.shape[0]
    slot = units if units % 8 == 0 else -(-units // 16) * 16
    d = Dims(n, planes, height, units, slot, width, group)
    j = lax.axis_index(seq)
    z = lax.axis_index("plane")
    c = lax.axis_index("core")
    info = jnp.concatenate([jnp.stack([j, z, c]).astype(jnp.int32), doc_starts[0]])

    def swap(a):
        return lax.ppermute(a, "core", [(0, 1), (1, 0)])

    def around(a, k):
        return lax.ppermute(a, seq, [(t, t ^ k) for t in range(n)])

    def across(a, k):
        return lax.ppermute(a, "plane", [(t, t ^ k) for t in range(planes)])

    def gather_seq(a):
        return [a] + [around(a, k) for k in range(1, n)]

    def between(a, pairs):
        return lax.ppermute(a, ("plane", "core"), pairs)

    def gather_planes(a):
        if planes != 4:
            return [(a,)] + [(across(a, k),) for k in range(1, planes)]
        pair = across(a, 1)
        mid = between(a, MIDDLE)
        far = across(mid, 1)
        near = between(pair, MIDDLE)
        last = between(pair, LAST)
        return [(a,), (pair,), (far, near), (last, mid)]

    def both_cores(blocks):
        return [b for ways in blocks for a in ways for b in (a, swap(a))]

    def send_seq(own, sends):
        return [own] + [around(a, k + 1) for k, a in enumerate(sends)]

    def send_planes(own, sends):
        return [own] + [across(a, k + 1) for k, a in enumerate(sends)]

    def to_all(blocks):
        axes = ("plane",) + seq
        return lax.all_to_all(blocks, axes, split_axis=0, concat_axis=0, tiled=True)

    def run(kernel, outs, args, **kw):
        return call(kernel, outs, args, **kw)

    half = HEAD_DIM // 2
    freq = 10000.0 ** (-(jnp.arange(half, dtype=f32) * 2.0) / HEAD_DIM)
    lane_freq = jnp.concatenate([freq] * (128 // half))
    angle = jnp.arange(length, dtype=f32)[:, None] * lane_freq[None, :]
    cosine, sine = jnp.cos(angle), jnp.sin(angle)

    (rows_pack,) = run(
        pack_kernel, [out((height + units, width), bf16)], [w_out, w_down], smem=0, limit=60
    )
    row_planes = gather_planes(rows_pack)
    pieces = run(
        functools.partial(split_kernel, d),
        [out(((d.tiles + d.in_tiles) * height, 128), bf16)] * n,
        [info, w_query, w_key, w_value, w_gate, w_up],
        scratch=[pltpu.VMEM((height, d.wide), bf16)] * 2,
        limit=60,
    )
    in_payload, gu_payload = run(
        functools.partial(place_kernel, d),
        [out((d.in_tiles * strip, 128), bf16), out((d.gu_rows, 128), bf16)],
        [info, *send_seq(pieces[0], pieces[1:])],
    )
    xs = gather_seq(x)
    in_blocks = both_cores(gather_planes(in_payload))
    gu_blocks = both_cores(gather_planes(gu_payload))
    row_blocks = both_cores(row_planes)
    ogs = gather_seq(og)
    outer = (z == 0) | (z == planes - 1)
    out_planes = jnp.stack(
        [
            jnp.where(outer, a[0][:height], a[1][:height]) if len(a) > 1 else a[0][:height]
            for a in row_planes
        ]
    )
    out_parts = [b for a in gather_seq(out_planes) for b in (a, swap(a))]
    (out_mat,) = run(
        functools.partial(out_mat_kernel, n, planes),
        [out((width, width), bf16)],
        [info, *out_parts],
    )

    normed, qkv_mat, qkv, lse, context = run(
        functools.partial(attend_kernel, d, docs),
        [
            out((length, width), bf16),
            out((width, 3 * group), bf16),
            out((length, 3 * group), bf16),
            out((length, HEADS // n), f32),
            out((length, group), bf16),
        ],
        [info, *xs, *in_blocks, cosine, sine],
        flops=8 * length * width * group,
    )
    contexts = gather_seq(context)
    resid, normed2 = run(
        functools.partial(project_kernel, n),
        [out((tokens, width), f32), out((length, width), bf16)],
        [info, *contexts, out_mat, *xs],
        scratch=[pltpu.VMEM((length, width), f32)],
        flops=2 * length * width * width,
    )
    block_f = out((tokens, width), f32)
    block_l = out((tokens, width), bf16)
    cols = d.tiles * 128
    hidden, d_gu, dn_own, *rest = run(
        functools.partial(ffn_kernel, d),
        [out((length, d.wide), bf16), out((length, cols), bf16), block_f]
        + [block_l] * (n - 1)
        + [out((d.wide, width), bf16), out((length, width), bf16)],
        [info, normed2, *gu_blocks, *row_blocks, *ogs],
        scratch=[pltpu.VMEM((width, cols), bf16), pltpu.VMEM((length, width), f32)],
        flops=10 * length * width * d.ff,
    )
    dn_parts = send_seq(dn_own, rest[: n - 1])
    down_mat, og_full = rest[n - 1 :]

    keep, send = run(
        functools.partial(ffn_send_kernel, d),
        [out((planes, slot, width), f32), out((planes, d.payload, 128), bf16)],
        [info, normed2, d_gu, hidden, og_full],
        scratch=[pltpu.VMEM((length, width // 2), bf16), pltpu.VMEM((d.wide, width), f32)],
        flops=4 * length * width * d.ff,
    )
    own_gu, own_down, *sends = run(
        functools.partial(ffn_split_kernel, d),
        [out((strip, cols), f32), out((slot, width), f32)]
        + [out((d.payload, 128), bf16)] * (planes - 1),
        [info, normed2, d_gu, keep, swap(send)],
        scratch=[pltpu.VMEM((length, width // 2), bf16), pltpu.VMEM((width // 2, cols), f32)],
        flops=2 * length * width * d.ff,
    )
    if planes == 4:
        near, two, far = sends
        parts = [across(two, 1), between(two, MIDDLE), between(far, FIRST)]
        to_pair, to_mid = run(
            ffn_mid_kernel, [out((d.payload, 128), bf16)] * 2, [info, near, far, *parts]
        )
        ffn_parts = [across(to_pair, 1), between(to_mid, MIDDLE)]
    else:
        ffn_parts = [across(a, k + 1) for k, a in enumerate(sends)]
    grad_down, *pieces = run(
        functools.partial(ffn_sum_kernel, d),
        [out(w_down.shape, f32)] + [out((d.tiles * height, 128), bf16)] * n,
        [info, own_gu, own_down, *ffn_parts],
        scratch=[pltpu.VMEM((strip, 128), f32)],
    )
    grad_gate, grad_up = run(
        functools.partial(join_kernel, d),
        [out(w_gate.shape, f32)] * 2,
        [info, *send_seq(pieces[0], pieces[1:])],
        scratch=[pltpu.VMEM((height, d.wide), f32)] * 2,
    )

    d_resid, d_branch, *pieces = run(
        functools.partial(resid_back_kernel, n),
        [block_f, block_l] + [out((tokens, group), bf16)] * n,
        [info, *dn_parts, resid, og, out_mat],
        scratch=[pltpu.VMEM((tokens, width), f32)],
        flops=2 * tokens * width * width,
    )
    ho_own, *sends = run(
        functools.partial(hidden_out_kernel, n),
        [block_f] + [out((2 * tokens, width), bf16)] * (n - 1),
        [info, hidden, down_mat, d_branch],
        scratch=[pltpu.VMEM((length, width), f32)],
        flops=2 * length * width * d.ff,
    )
    ho_parts = [around(a, k + 1) for k, a in enumerate(sends)]
    (hidden_out,) = run(hidden_sum_kernel, [block_l], [resid, ho_own, *ho_parts], smem=0)
    d_qkv, n1_own, *sends = run(
        functools.partial(attend_back_kernel, n, docs),
        [out((length, 3 * group), bf16), block_f] + [block_l] * (n - 1),
        [info, *send_seq(pieces[0], pieces[1:]), qkv, lse, qkv_mat, cosine, sine],
        scratch=[pltpu.VMEM((length, group), f32)] * 3
        + [pltpu.VMEM((length, group), bf16), pltpu.VMEM((length, width), f32)],
        flops=12 * length * width * group,
    )
    n1_parts = send_seq(n1_own, sends)
    (in_grad,) = run(
        functools.partial(input_back_kernel, n), [block_f], [*n1_parts, x, d_resid], smem=0
    )
    picked = [pltpu.VMEM((length, width // 2), bf16)]
    in_half = out((planes, strip, 3 * group), bf16)
    flops = 3 * length * width * group
    (send,) = run(grad_send_kernel, [in_half], [info, normed, d_qkv], scratch=picked, flops=flops)
    args = [info, normed, d_qkv, swap(send)]
    (in_sum,) = run(grad_all_kernel, [in_half], args, scratch=picked, flops=flops)
    in_sum = to_all(in_sum.reshape(planes * n, height, 3 * group))
    in_grads = run(
        functools.partial(sum_in_kernel, n), [out(w_query.shape, f32)] * 3, [in_sum], smem=0
    )
    keep, send = run(
        functools.partial(grad_out_kernel, n),
        [out((planes, height, width), f32), out((planes, height, width), bf16)],
        [info, *contexts, d_branch, *ho_parts],
        scratch=[
            pltpu.VMEM((width, length), f32),
            pltpu.VMEM((2 * planes * height, length), f32),
            pltpu.VMEM((length, width), bf16),
        ],
        flops=2 * length * group * width,
    )
    own, *sends = run(
        add_split_kernel,
        [out((height, width), f32)] + [out((height, width), bf16)] * (planes - 1),
        [info, keep, swap(send)],
    )
    parts = send_planes(own, sends)
    (grad_out,) = run(sum_kernel, [out(w_out.shape, f32)], parts, smem=0)
    return (
        hidden_out[None], in_grad[None], *in_grads, grad_out, grad_gate, grad_up, grad_down
    )


def solution(mesh):
    dp, seq = mesh.shape["dp"], mesh.shape["seq"]
    fine = Mesh(
        mesh.devices.reshape(dp // 2, 2, seq // 2, 2), ("plane", "core", "seq_hi", "seq_lo")
    )
    token = P(("plane", "core"), ("seq_hi", "seq_lo"), None)
    weight = P(("plane", "core", "seq_hi", "seq_lo"), None)
    return jax.shard_map(
        layer,
        mesh=fine,
        in_specs=(token, P(("plane", "core"), None)) + (weight,) * 7 + (token,),
        out_specs=(token, token) + (weight,) * 7,
        check_vma=False,
    )
```

```python
import functools
import typing

import jax
import jax.numpy as jnp
from jax import lax
from jax.experimental import pallas as pl
from jax.experimental.pallas import tpu as pltpu
from jax.sharding import Mesh, PartitionSpec as P


HEADS = 16
HEAD_DIM = 64
eps = 1e-05
bf16 = jnp.bfloat16
f32 = jnp.float32
NN = (((1,), (0,)), ((), ()))
NT = (((1,), (1,)), ((), ()))
TN = (((0,), (0,)), ((), ()))


def dot(left, right, dims=NN):
    return lax.dot_general(left, right, dims, preferred_element_type=f32)


def rows(start, size):
    return pl.ds(pl.multiple_of(start, size), size)


def norm_parts(values):
    centred = values - jnp.mean(values, axis=-1, keepdims=True)
    inv = lax.rsqrt(jnp.mean(centred * centred, axis=-1, keepdims=True) + eps)
    return centred * inv, inv


def norm_back(normed, inv, grad):
    mean_grad = jnp.mean(grad, axis=-1, keepdims=True)
    mean_both = jnp.mean(grad * normed, axis=-1, keepdims=True)
    return (grad - mean_grad - normed * mean_both) * inv


SEQ = ("seq_hi", "seq_lo")


def located(kernel, starts):
    def body(*refs):
        spot = [lax.axis_index(SEQ), lax.axis_index("plane"), lax.axis_index("core")]
        if starts:
            spot += [refs[0][0, t] for t in range(refs[0].shape[1])]
        kernel(spot, *refs[starts:])

    return body


def call(kernel, outs, args, scratch=(), flops=0, starts=0, spot=True, limit=24):
    vmem = pl.BlockSpec(memory_space=pltpu.VMEM)
    in_specs = [pl.BlockSpec(memory_space=pltpu.SMEM)] * starts + [vmem] * (len(args) - starts)
    moved = sum(a.size * a.dtype.itemsize for a in args) + sum(
        o.size * jnp.dtype(o.dtype).itemsize for o in outs
    )
    return pl.pallas_call(
        located(kernel, starts) if spot else kernel,
        out_shape=outs,
        in_specs=in_specs,
        out_specs=[vmem] * len(outs),
        scratch_shapes=list(scratch),
        cost_estimate=pl.CostEstimate(flops=flops, bytes_accessed=moved, transcendentals=0),
        compiler_params=pltpu.CompilerParams(vmem_limit_bytes=limit * 1024 * 1024),
    )(*args)


def out(shape, dtype):
    return jax.ShapeDtypeStruct(shape, dtype)


def turn(values, cosine, sine, sign):
    width = values.shape[-1]
    half = HEAD_DIM // 2
    lane = lax.broadcasted_iota(jnp.int32, values.shape, 1)
    first = (lane & (HEAD_DIM - 1)) < half
    ahead = pltpu.roll(values, width - half, 1)
    behind = pltpu.roll(values, half, 1)
    other = jnp.where(first, -ahead, behind)
    return values * cosine + (other * sine if sign > 0 else -(other * sine))


def head_lanes(shape, head):
    lane = lax.broadcasted_iota(jnp.int32, shape, 1)
    return (lane >= head * HEAD_DIM) & (lane < (head + 1) * HEAD_DIM)


def masked(scores, starts, first_row):
    pos = lax.broadcasted_iota(jnp.int32, (scores.shape[0], 1), 0) + first_row
    begin = jnp.zeros_like(pos)
    for start in starts:
        begin = jnp.where(pos >= start, start, begin)
    keys = lax.broadcasted_iota(jnp.int32, scores.shape, 1)
    return jnp.where((keys >= begin) & (keys <= pos), scores, -1e30)


def attend_kernel(d, docs, info, *refs):
    n = d.n
    count = 2 * sum(ways(d.planes))
    xs, blocks = refs[:n], refs[n : n + count]
    cos_ref, sin_ref, normed, mats, qkv, lse, context = refs[n + count :]
    j = info[0]
    tokens = xs[0].shape[0]
    for k in range(n):
        block, _ = norm_parts(xs[k][...].astype(f32))
        normed[rows((j ^ k) * tokens, tokens), :] = block.astype(bf16)

    def put(block, source):
        here = rows(block * d.strip, d.strip)
        for t in range(d.in_tiles):
            mats[here, t * 128 : (t + 1) * 128] = source[t * d.strip : (t + 1) * d.strip, :]

    each_block(d, info, blocks, put)
    pre = dot(normed[...], mats[...])
    width = pre.shape[1] // 3
    reps = width // cos_ref.shape[1]
    cosine = jnp.concatenate([cos_ref[...]] * reps, axis=1)
    sine = jnp.concatenate([sin_ref[...]] * reps, axis=1)
    qkv[:, :width] = (
        turn(pre[:, :width], cosine, sine, 1).astype(bf16).astype(f32) * HEAD_DIM**-0.5
    ).astype(bf16)
    qkv[:, width : 2 * width] = turn(pre[:, width : 2 * width], cosine, sine, 1).astype(bf16)
    qkv[:, 2 * width :] = pre[:, 2 * width :].astype(bf16)
    starts = [info[3 + d] for d in range(docs)]
    length = qkv.shape[0]
    step = 256

    for b in range(length // step):
        here, upto = slice(b * step, (b + 1) * step), slice(0, (b + 1) * step)
        query = qkv[here, :width]
        total = jnp.zeros((step, width), f32)
        for head in range(width // HEAD_DIM):
            mine = head_lanes(query.shape, head)
            scores = dot(jnp.where(mine, query, 0), qkv[upto, width : 2 * width], NT)
            scores = masked(scores, starts, b * step)
            top = jnp.max(scores, axis=-1, keepdims=True)
            expo = jnp.exp(scores - top)
            mass = jnp.sum(expo, axis=-1, keepdims=True)
            probs = (expo * (1.0 / mass)).astype(bf16)
            total = jnp.where(mine, dot(probs, qkv[upto, 2 * width :]), total)
            lse[here, head : head + 1] = top + jnp.log(mass)
        context[here, :] = total.astype(bf16)


class Dims(typing.NamedTuple):
    n: int
    planes: int
    height: int
    units: int
    slot: int
    width: int
    group: int

    @property
    def strip(self):
        return self.n * self.height

    @property
    def ff(self):
        return 2 * self.planes * self.slot

    @property
    def whole(self):
        return self.ff // 128 if self.shared else -(-self.ff // 128)

    @property
    def shared(self):
        return self.ff % 128 == 64

    @property
    def tiles(self):
        return 2 * self.whole + self.shared

    @property
    def wide(self):
        return (self.whole + self.shared) * 128

    @property
    def gu_rows(self):
        return self.tiles * self.strip

    @property
    def in_tiles(self):
        return 3 * self.group // 128

    @property
    def payload(self):
        return self.gu_rows + self.width // 128 * self.slot


def ways(planes):
    return (1, 1, 2, 2) if planes == 4 else (1,) * planes


def each_block(d, info, refs, place):
    z, c = info[1], info[2]
    outer = (z == 0) | (z == d.planes - 1)
    at = 0
    for k, count in enumerate(ways(d.planes)):
        for a in range(count):
            for m in range(2):
                put = functools.partial(place, 2 * (z ^ k) + (c ^ m), refs[at])
                at += 1
                if count == 1:
                    put()
                else:
                    pl.when(outer if a == 0 else jnp.logical_not(outer))(put)


def gate_up_tile(d, gate, up, t):
    if t < d.whole:
        return gate[:, t * 128 : (t + 1) * 128]
    if t < 2 * d.whole:
        return up[:, (t - d.whole) * 128 : (t - d.whole + 1) * 128]
    at = d.whole * 128
    return jnp.concatenate([gate[:, at : at + 64], up[:, at : at + 64]], axis=1)


def split_kernel(d, info, *refs):
    mats, (w_gate, w_up), pieces = refs[:3], refs[3:5], refs[5 : 5 + d.n]
    gate, up = refs[5 + d.n :]
    if d.slot > d.units:
        gate[...] = jnp.zeros_like(gate)
        up[...] = jnp.zeros_like(up)
    for group in range(d.n):
        for b in range(2 * d.planes):
            here = (b * d.n + group) * d.units
            there = slice(b * d.slot, b * d.slot + d.units)
            gate[:, there] = w_gate[:, here : here + d.units]
            up[:, there] = w_up[:, here : here + d.units]
        for k in range(d.n):

            @pl.when((info[0] ^ k) == group)
            def unused(group=group, k=k):
                for t in range(d.tiles):
                    tile = gate_up_tile(d, gate, up, t)
                    pieces[k][t * d.height : (t + 1) * d.height, :] = tile
                for t in range(d.in_tiles):
                    at = d.tiles + t
                    which, lane = divmod(t * 128, d.group)
                    lane += group * d.group
                    pieces[k][at * d.height : (at + 1) * d.height, :] = mats[which][
                        :, lane : lane + 128
                    ]


def place_kernel(d, info, *refs):
    pieces, (in_payload, gu_payload) = refs[: d.n], refs[d.n :]
    for k in range(d.n):
        for t in range(d.tiles + d.in_tiles):
            inner = t >= d.tiles
            at = (t - d.tiles if inner else t) * d.strip + (info[0] ^ k) * d.height
            piece = pieces[k][t * d.height : (t + 1) * d.height, :]
            (in_payload if inner else gu_payload)[rows(at, d.height), :] = piece


def join_kernel(d, info, *refs):
    pieces, (grad_gate, grad_up, gate, up) = refs[: d.n], refs[d.n :]
    for group in range(d.n):
        for k in range(d.n):

            @pl.when((info[0] ^ k) == group)
            def unused(k=k):
                for t in range(d.tiles):
                    tile = pieces[k][t * d.height : (t + 1) * d.height, :].astype(f32)
                    if t < d.whole:
                        gate[:, t * 128 : (t + 1) * 128] = tile
                    elif t < 2 * d.whole:
                        up[:, (t - d.whole) * 128 : (t - d.whole + 1) * 128] = tile
                    else:
                        gate[:, d.whole * 128 : d.whole * 128 + 64] = tile[:, :64]
                        up[:, d.whole * 128 : d.whole * 128 + 64] = tile[:, 64:]

        for b in range(2 * d.planes):
            there = (b * d.n + group) * d.units
            here = slice(b * d.slot, b * d.slot + d.units)
            grad_gate[:, there : there + d.units] = gate[:, here]
            grad_up[:, there : there + d.units] = up[:, here]


def out_mat_kernel(n, planes, info, *refs):
    parts, (whole,) = refs[:-1], refs[-1:]
    j, z, c = info[0], info[1], info[2]
    size = parts[0].shape[1]
    for p in range(n):
        for m in range(2):
            for k in range(planes):
                at = ((2 * (z ^ k) + (c ^ m)) * n + (j ^ p)) * size
                whole[rows(at, size), :] = parts[2 * p + m][k]


def project_kernel(n, info, *refs):
    contexts = refs[:n]
    mats = refs[n]
    xs = refs[n + 1 : 2 * n + 1]
    resid_own, normed, acc = refs[2 * n + 1 :]
    j = info[0]
    width = contexts[0].shape[1]
    tokens = xs[0].shape[0]
    acc[...] = dot(contexts[0][...], mats[rows(j * width, width), :])
    for p in range(1, n):
        acc[...] += dot(contexts[p][...], mats[rows((j ^ p) * width, width), :])
    for k in range(n):
        here = rows((j ^ k) * tokens, tokens)
        resid = xs[k][...].astype(f32) + acc[here, :]
        if k == 0:
            resid_own[...] = resid
        normed[here, :] = norm_parts(resid)[0].astype(bf16)


def gate_part(d, both):
    if d.shared:
        at = 2 * d.whole * 128
        return jnp.concatenate([both[:, : d.whole * 128], both[:, at:]], axis=1)
    return both[:, : d.whole * 128]


def up_part(d, both):
    at = d.whole * 128
    if d.shared:
        last = pltpu.roll(both[:, 2 * at :], 64, 1)
        return jnp.concatenate([both[:, at : 2 * at], last], axis=1)
    return both[:, at:]


def ffn_kernel(d, info, normed, *refs):
    count = 2 * sum(ways(d.planes))
    blocks, downs = refs[:count], refs[count : 2 * count]
    grads = refs[2 * count : 2 * count + d.n]
    hidden, d_gu, own_grad, *rest = refs[2 * count + d.n :]
    sends = rest[: d.n - 1]
    down_mat, og_full, gu_mat, acc = rest[d.n - 1 :]
    j = info[0]
    tokens = grads[0].shape[0]
    if d.slot > d.units:
        down_mat[...] = jnp.zeros_like(down_mat)
    elif d.wide > d.ff:
        down_mat[d.ff :, :] = jnp.zeros((d.wide - d.ff, d.width), bf16)

    def put_gu(block, source):
        here = rows(block * d.strip, d.strip)
        for t in range(d.tiles):
            gu_mat[here, t * 128 : (t + 1) * 128] = source[t * d.strip : (t + 1) * d.strip, :]

    def put_down(block, source):
        at = pl.multiple_of(block * d.slot, d.slot)
        down_mat[pl.ds(at, d.units), :] = source[...]

    each_block(d, info, blocks, put_gu)
    each_block(d, info, downs, put_down)
    for k in range(d.n):
        og_full[rows((j ^ k) * tokens, tokens), :] = grads[k][...]
    both = dot(normed[...], gu_mat[...])
    d_hidden = dot(og_full[...], down_mat[...], NT)
    gate, up = gate_part(d, both), up_part(d, both)
    sig = 1.0 / (1.0 + jnp.exp(-gate))
    silu = gate * sig
    mixed = silu * up
    d_gate = d_hidden * up * (sig + gate * sig * (1.0 - sig))
    d_up = d_hidden * silu
    at = d.whole * 128
    if d.shared:
        lane = lax.broadcasted_iota(jnp.int32, (mixed.shape[0], 128), 1)
        hidden[:, :at] = mixed[:, :at].astype(bf16)
        hidden[:, at:] = jnp.where(lane < 64, mixed[:, at:], 0.0).astype(bf16)
        last = jnp.where(lane < 64, d_gate[:, at:], pltpu.roll(d_up[:, at:], 64, 1))
        d_gu[:, 2 * at :] = last.astype(bf16)
    else:
        hidden[...] = mixed.astype(bf16)
    d_gu[:, :at] = d_gate[:, :at].astype(bf16)
    d_gu[:, at : 2 * at] = d_up[:, :at].astype(bf16)
    acc[...] = dot(d_gu[...], gu_mat[...], NT)
    own_grad[...] = acc[rows(j * tokens, tokens), :]
    for k in range(1, d.n):
        sends[k - 1][...] = acc[rows((j ^ k) * tokens, tokens), :].astype(bf16)


def hidden_out_kernel(n, info, left, right, branch, own, *rest):
    sends, acc = rest[:-1], rest[-1]
    j = info[0]
    tokens = own.shape[0]
    acc[...] = dot(left[...], right[...])
    own[...] = acc[rows(j * tokens, tokens), :]
    for k in range(1, n):
        sends[k - 1][:tokens, :] = acc[rows((j ^ k) * tokens, tokens), :].astype(bf16)
        sends[k - 1][tokens:, :] = branch[...]


def hidden_sum_kernel(resid, own, *refs):
    total = resid[...] + own[...]
    for part in refs[:-1]:
        total = total + part[: own.shape[0], :].astype(f32)
    refs[-1][...] = total.astype(bf16)


def resid_back_kernel(n, info, *refs):
    parts = refs[:n]
    resid, out_grad, mats, d_resid, d_branch, *pieces, acc = refs[n:]
    grad = parts[0][...]
    for part in parts[1:]:
        grad = grad + part[...].astype(f32)
    normed, inv = norm_parts(resid[...])
    total = out_grad[...].astype(f32) + norm_back(normed, inv, grad)
    d_resid[...] = total
    d_branch[...] = total.astype(bf16)
    acc[...] = dot(total.astype(bf16), mats[...], NT)
    width = pieces[0].shape[1]
    for k in range(n):
        pieces[k][...] = acc[:, rows((info[0] ^ k) * width, width)].astype(bf16)


def input_back_kernel(n, *refs):
    parts = refs[:n]
    x, d_resid, in_grad = refs[n:]
    grad = parts[0][...]
    for part in parts[1:]:
        grad = grad + part[...].astype(f32)
    normed, inv = norm_parts(x[...].astype(f32))
    in_grad[...] = d_resid[...] + norm_back(normed, inv, grad)


def attend_back_kernel(n, docs, info, *refs):
    pieces = refs[:n]
    qkv, lse, mats, cos_ref, sin_ref = refs[n : n + 5]
    d_qkv, own, *rest = refs[n + 5 :]
    sends = rest[: n - 1]
    d_key, d_value, d_query, d_contexts, acc = rest[n - 1 :]
    j = info[0]
    tokens, width = pieces[0].shape
    for k in range(n):
        d_contexts[rows((j ^ k) * tokens, tokens), :] = pieces[k][...]
    length = qkv.shape[0]
    starts = [info[3 + d] for d in range(docs)]
    step = 256
    d_key[...] = jnp.zeros_like(d_key)
    d_value[...] = jnp.zeros_like(d_value)

    for b in range(length // step):
        here, upto = slice(b * step, (b + 1) * step), slice(0, (b + 1) * step)
        d_context = d_contexts[here, :]
        query = qkv[here, :width]
        keys = qkv[upto, width : 2 * width]
        d_q = jnp.zeros((step, width), f32)
        for head in range(width // HEAD_DIM):
            lanes = head_lanes(query.shape, head)
            q_head = jnp.where(lanes, query, 0)
            g_head = jnp.where(lanes, d_context, 0)
            scores = masked(dot(q_head, keys, NT), starts, b * step)
            probs = jnp.exp(scores - lse[here, head : head + 1])
            d_probs = dot(g_head, qkv[upto, 2 * width :], NT)
            delta = jnp.sum(probs * d_probs, axis=-1, keepdims=True)
            d_scores = (probs * (d_probs - delta)).astype(bf16)
            d_value[upto, :] += dot(probs.astype(bf16), g_head, TN)
            d_key[upto, :] += dot(d_scores, q_head, TN)
            d_q = jnp.where(lanes, dot(d_scores, keys), d_q)
        d_query[here, :] = d_q * HEAD_DIM**-0.5

    reps = width // cos_ref.shape[1]
    cosine = jnp.concatenate([cos_ref[...]] * reps, axis=1)
    sine = jnp.concatenate([sin_ref[...]] * reps, axis=1)
    low_q = d_query[...].astype(bf16).astype(f32)
    low_k = d_key[...].astype(bf16).astype(f32)
    d_qkv[:, :width] = turn(low_q, cosine, sine, -1).astype(bf16)
    d_qkv[:, width : 2 * width] = turn(low_k, cosine, sine, -1).astype(bf16)
    d_qkv[:, 2 * width :] = d_value[...].astype(bf16)
    acc[...] = dot(d_qkv[...], mats[...], NT)
    own[...] = acc[rows(j * tokens, tokens), :]
    for k in range(1, n):
        sends[k - 1][...] = acc[rows((j ^ k) * tokens, tokens), :].astype(bf16)


def pick_lanes(left, picked, core, planes):
    size = left.shape[1] // (2 * planes)
    for z in range(planes):
        if size % 128:
            low = left[:, 2 * z * size : (2 * z + 1) * size]
            high = left[:, (2 * z + 1) * size : (2 * z + 2) * size]
            picked[:, z * size : (z + 1) * size] = jnp.where(core == 0, low, high)
        else:
            picked[:, z * size : (z + 1) * size] = left[:, rows((2 * z + core) * size, size)]


def grad_send_kernel(info, left, right, send, picked):
    planes, size = send.shape[0], send.shape[1]
    pick_lanes(left, picked, 1 - info[2], planes)
    product = dot(picked[...], right[...], TN)
    for z in range(planes):
        send[z] = product[z * size : (z + 1) * size].astype(bf16)


def grad_all_kernel(info, left, right, got, total, picked):
    planes, size = got.shape[0], got.shape[1]
    pick_lanes(left, picked, info[2], planes)
    product = dot(picked[...], right[...], TN)
    for z in range(planes):
        total[z] = (product[z * size : (z + 1) * size] + got[z].astype(f32)).astype(bf16)


def parts_of(planes):
    return ((2, 3), (0, 1)) if planes == 4 else (tuple(range(1, planes)), (0,))


def pick_blocks(left, picked, core, z, ks):
    size = picked.shape[1] // len(ks)
    for at, k in enumerate(ks):
        if size % 128:
            both = left[:, rows((z ^ k) * 2 * size, 2 * size)]
            block = jnp.where(core == 0, both[:, :size], both[:, size:])
        else:
            block = left[:, rows((2 * (z ^ k) + core) * size, size)]
        picked[:, at * size : (at + 1) * size] = block


def ffn_send_kernel(d, ks, info, normed, d_gu, *refs):
    z, c = info[1], info[2]
    if len(refs) > 3:
        hidden, og_full, down, send, picked = refs
        down[...] = dot(hidden[...], og_full[...], TN)
    else:
        down, send, picked = refs
    pick_blocks(normed, picked, 1 - c, z, ks)
    product = dot(picked[...], d_gu[...], TN).astype(bf16)
    for at, k in enumerate(ks):
        for t in range(d.tiles):
            send[at, t * d.strip : (t + 1) * d.strip, :] = product[
                at * d.strip : (at + 1) * d.strip, t * 128 : (t + 1) * 128
            ]
        other = down[rows((2 * (z ^ k) + 1 - c) * d.slot, d.slot), :].astype(bf16)
        for t in range(d.width // 128):
            row = d.gu_rows + t * d.slot
            send[at, row : row + d.slot, :] = other[:, t * 128 : (t + 1) * 128]


def ffn_split_kernel(d, ks, info, normed, d_gu, down, got, *refs):
    outs, (picked, acc) = refs[:-2], refs[-2:]
    z, c = info[1], info[2]
    pick_blocks(normed, picked, c, z, ks)
    acc[...] = dot(picked[...], d_gu[...], TN)
    for at, k in enumerate(ks):
        mine = down[rows((2 * (z ^ k) + c) * d.slot, d.slot), :]
        for t in range(d.tiles):
            here, lanes = slice(t * d.strip, (t + 1) * d.strip), slice(t * 128, (t + 1) * 128)
            total = acc[at * d.strip : (at + 1) * d.strip, lanes] + got[at, here, :].astype(f32)
            if k:
                outs[at - len(ks)][here, :] = total.astype(bf16)
            else:
                outs[0][:, lanes] = total
        for t in range(d.width // 128):
            here = slice(d.gu_rows + t * d.slot, d.gu_rows + (t + 1) * d.slot)
            lanes = slice(t * 128, (t + 1) * 128)
            total = mine[:, lanes] + got[at, here, :].astype(f32)
            if k:
                outs[at - len(ks)][here, :] = total.astype(bf16)
            else:
                outs[1][:, lanes] = total


def ffn_mid_kernel(info, near, far, *refs):
    (first, second, third), (to_pair, to_mid) = refs[:3], refs[3:]
    inner = (info[1] == 1) | (info[1] == 2)
    passed = jnp.where(inner, second[...].astype(f32) + third[...].astype(f32), 0.0)
    to_pair[...] = (near[...].astype(f32) + passed).astype(bf16)
    to_mid[...] = (far[...].astype(f32) + first[...].astype(f32)).astype(bf16)


def ffn_sum_kernel(d, info, own_gu, own_down, *refs):
    count = 2 if d.planes == 4 else d.planes - 1
    parts = refs[:count]
    grad_down, *pieces, acc = refs[count:]
    inner = (info[1] == 1) | (info[1] == 2)

    def add(total, here):
        for k, part in enumerate(parts):
            block = part[here, :].astype(f32)
            total = total + (jnp.where(inner, block, 0.0) if k and d.planes == 4 else block)
        return total

    for t in range(d.tiles):
        acc[...] = add(own_gu[:, t * 128 : (t + 1) * 128], slice(t * d.strip, (t + 1) * d.strip))
        for k in range(d.n):
            pieces[k][t * d.height : (t + 1) * d.height, :] = acc[
                rows((info[0] ^ k) * d.height, d.height), :
            ].astype(bf16)
    for t in range(d.width // 128):
        at, lanes = d.gu_rows + t * d.slot, slice(t * 128, (t + 1) * 128)
        grad_down[:, lanes] = add(own_down[: d.units, lanes], slice(at, at + d.units))


def add_split_kernel(info, keep, got, own, *sends):
    z = info[1]
    own[...] = keep[z] + got[z].astype(f32)
    for k in range(1, keep.shape[0]):
        sends[k - 1][...] = (keep[z ^ k] + got[z ^ k].astype(f32)).astype(bf16)


def sum_kernel(*refs):
    total = refs[0][...]
    for part in refs[1:-1]:
        total = total + part[...].astype(f32)
    refs[-1][...] = total


def sum_in_kernel(n, parts, *grads):
    planes = parts.shape[0] // n
    width = parts.shape[2] // 3
    for group in range(n):
        total = parts[group].astype(f32)
        for z in range(1, planes):
            total = total + parts[z * n + group].astype(f32)
        for t in range(3):
            grads[t][:, group * width : (group + 1) * width] = total[:, t * width : (t + 1) * width]


def grad_out_kernel(n, info, *refs):
    contexts, branches = refs[:n], refs[n : 2 * n]
    keep, send, turned, left, right = refs[2 * n :]
    j, c = info[0], info[2]
    width = contexts[0].shape[1]
    tokens = branches[0].shape[0]
    for p in range(n):
        block = branches[p][tokens:, :] if p else branches[p][...]
        right[rows((j ^ p) * tokens, tokens), :] = block
        turned[rows((j ^ p) * width, width), :] = contexts[p][...].astype(f32).T
    planes, height = keep.shape[0], keep.shape[1]
    block = height * n
    for m in range(2):
        for z in range(planes):
            at = (2 * z + (c ^ m)) * block + j * height
            left[pl.ds((m * planes + z) * height, height), :] = turned[
                pl.ds(pl.multiple_of(at, height), height), :
            ]
    product = dot(left[...].astype(bf16), right[...])
    for z in range(planes):
        keep[z] = product[z * height : (z + 1) * height]
        send[z] = product[(planes + z) * height : (planes + z + 1) * height].astype(bf16)


MIDDLE = ((2, 4), (3, 5), (4, 2), (5, 3), (0, 1), (1, 0), (6, 7), (7, 6))
LAST = tuple((2 * a + t, 2 * b + t) for a, b in ((1, 3), (2, 0), (0, 1), (3, 2)) for t in range(2))
FIRST = tuple((b, a) for a, b in LAST)


def layer(hidden_in, doc_starts, w_query, w_key, w_value, w_out, w_gate, w_up, w_down, out_grad):
    x = hidden_in[0]
    og = out_grad[0]
    tokens, width = x.shape
    seq = SEQ
    n = lax.axis_size(seq)
    planes = lax.axis_size("plane")
    length = tokens * n
    group = HEADS // n * HEAD_DIM
    docs = doc_starts.shape[1]
    height = w_query.shape[0]
    strip = n * height
    units = w_down.shape[0]
    slot = units if units % 8 == 0 else -(-units // 16) * 16
    d = Dims(n, planes, height, units, slot, width, group)
    z = lax.axis_index("plane")

    def swap(a):
        return lax.ppermute(a, "core", [(0, 1), (1, 0)])

    def around(a, k):
        return lax.ppermute(a, seq, [(t, t ^ k) for t in range(n)])

    def across(a, k):
        return lax.ppermute(a, "plane", [(t, t ^ k) for t in range(planes)])

    def gather_seq(a):
        return [a] + [around(a, k) for k in range(1, n)]

    def between(a, pairs):
        return lax.ppermute(a, ("plane", "core"), pairs)

    def gather_planes(a):
        if planes != 4:
            return [(a,)] + [(across(a, k),) for k in range(1, planes)]
        pair = across(a, 1)
        mid = between(a, MIDDLE)
        far = across(mid, 1)
        near = between(pair, MIDDLE)
        last = between(pair, LAST)
        return [(a,), (pair,), (far, near), (last, mid)]

    def both_cores(blocks):
        return [b for ways in blocks for a in ways for b in (a, swap(a))]

    def send_seq(own, sends):
        return [own] + [around(a, k + 1) for k, a in enumerate(sends)]

    def send_planes(own, sends):
        return [own] + [across(a, k + 1) for k, a in enumerate(sends)]

    def to_all(blocks):
        axes = ("plane",) + seq
        return lax.all_to_all(blocks, axes, split_axis=0, concat_axis=0, tiled=True)

    def run(kernel, outs, args, **kw):
        return call(kernel, outs, args, **kw)

    half = HEAD_DIM // 2
    freq = 10000.0 ** (-(jnp.arange(half, dtype=f32) * 2.0) / HEAD_DIM)
    lane_freq = jnp.concatenate([freq] * (128 // half))
    angle = jnp.arange(length, dtype=f32)[:, None] * lane_freq[None, :]
    cosine, sine = jnp.cos(angle), jnp.sin(angle)

    out_rows = gather_planes(w_out)
    pieces = run(
        functools.partial(split_kernel, d),
        [out(((d.tiles + d.in_tiles) * height, 128), bf16)] * n,
        [w_query, w_key, w_value, w_gate, w_up],
        scratch=[pltpu.VMEM((height, d.wide), bf16)] * 2,
        limit=60,
    )
    in_payload, gu_payload = run(
        functools.partial(place_kernel, d),
        [out((d.in_tiles * strip, 128), bf16), out((d.gu_rows, 128), bf16)],
        send_seq(pieces[0], pieces[1:]),
    )
    xs = gather_seq(x)
    in_blocks = both_cores(gather_planes(in_payload))
    gu_blocks = both_cores(gather_planes(gu_payload))
    row_blocks = both_cores(gather_planes(w_down))
    ogs = gather_seq(og)
    outer = (z == 0) | (z == planes - 1)
    out_planes = jnp.stack(
        [
            jnp.where(outer, a[0], a[1]) if len(a) > 1 else a[0] for a in out_rows
        ]
    )
    out_parts = [b for a in gather_seq(out_planes) for b in (a, swap(a))]
    (out_mat,) = run(
        functools.partial(out_mat_kernel, n, planes), [out((width, width), bf16)], [*out_parts]
    )

    normed, qkv_mat, qkv, lse, context = run(
        functools.partial(attend_kernel, d, docs),
        [
            out((length, width), bf16),
            out((width, 3 * group), bf16),
            out((length, 3 * group), bf16),
            out((length, HEADS // n), f32),
            out((length, group), bf16),
        ],
        [doc_starts, *xs, *in_blocks, cosine, sine],
        starts=1,
        flops=8 * length * width * group,
    )
    contexts = gather_seq(context)
    resid, normed2 = run(
        functools.partial(project_kernel, n),
        [out((tokens, width), f32), out((length, width), bf16)],
        [*contexts, out_mat, *xs],
        scratch=[pltpu.VMEM((length, width), f32)],
        flops=2 * length * width * width,
    )
    block_f = out((tokens, width), f32)
    block_l = out((tokens, width), bf16)
    cols = d.tiles * 128
    hidden, d_gu, dn_own, *rest = run(
        functools.partial(ffn_kernel, d),
        [out((length, d.wide), bf16), out((length, cols), bf16), block_f]
        + [block_l] * (n - 1)
        + [out((d.wide, width), bf16), out((length, width), bf16)],
        [normed2, *gu_blocks, *row_blocks, *ogs],
        scratch=[pltpu.VMEM((width, cols), bf16), pltpu.VMEM((length, width), f32)],
        flops=10 * length * width * d.ff,
    )
    dn_parts = send_seq(dn_own, rest[: n - 1])
    down_mat, og_full = rest[n - 1 :]

    down_grads, sent, outs = None, [], []
    for part, ks in enumerate(parts_of(planes)):
        payload = out((len(ks), d.payload, 128), bf16)
        args = [normed2, d_gu, down_grads] if part else [normed2, d_gu, hidden, og_full]
        *made, send = run(
            functools.partial(ffn_send_kernel, d, ks),
            [payload] if part else [out((d.wide, width), f32), payload],
            args,
            scratch=[pltpu.VMEM((length, len(ks) * strip), bf16)],
            flops=2 * length * len(ks) * strip * cols + (0 if part else 2 * length * d.ff * width),
        )
        down_grads = made[0] if made else down_grads
        sent.append(swap(send))
    for part, ks in enumerate(parts_of(planes)):
        owned = [out((strip, cols), f32), out((slot, width), f32)] if 0 in ks else []
        outs.append(
            run(
                functools.partial(ffn_split_kernel, d, ks),
                owned + [out((d.payload, 128), bf16)] * sum(k > 0 for k in ks),
                [normed2, d_gu, down_grads, sent[part]],
                scratch=[
                    pltpu.VMEM((length, len(ks) * strip), bf16),
                    pltpu.VMEM((len(ks) * strip, cols), f32),
                ],
                flops=2 * length * len(ks) * strip * cols,
            )
        )
    own_gu, own_down, *near = outs[1]
    sends = [*near, *outs[0]]
    if planes == 4:
        near, two, far = sends
        parts = [across(two, 1), between(two, MIDDLE), between(far, FIRST)]
        to_pair, to_mid = run(
            ffn_mid_kernel, [out((d.payload, 128), bf16)] * 2, [near, far, *parts]
        )
        ffn_parts = [across(to_pair, 1), between(to_mid, MIDDLE)]
    else:
        ffn_parts = [across(a, k + 1) for k, a in enumerate(sends)]
    grad_down, *pieces = run(
        functools.partial(ffn_sum_kernel, d),
        [out(w_down.shape, f32)] + [out((d.tiles * height, 128), bf16)] * n,
        [own_gu, own_down, *ffn_parts],
        scratch=[pltpu.VMEM((strip, 128), f32)],
    )
    grad_gate, grad_up = run(
        functools.partial(join_kernel, d),
        [out(w_gate.shape, f32)] * 2,
        [*send_seq(pieces[0], pieces[1:])],
        scratch=[pltpu.VMEM((height, d.wide), f32)] * 2,
    )

    d_resid, d_branch, *pieces = run(
        functools.partial(resid_back_kernel, n),
        [block_f, block_l] + [out((tokens, group), bf16)] * n,
        [*dn_parts, resid, og, out_mat],
        scratch=[pltpu.VMEM((tokens, width), f32)],
        flops=2 * tokens * width * width,
    )
    ho_own, *sends = run(
        functools.partial(hidden_out_kernel, n),
        [block_f] + [out((2 * tokens, width), bf16)] * (n - 1),
        [hidden, down_mat, d_branch],
        scratch=[pltpu.VMEM((length, width), f32)],
        flops=2 * length * width * d.ff,
    )
    ho_parts = [around(a, k + 1) for k, a in enumerate(sends)]
    (hidden_out,) = run(hidden_sum_kernel, [block_l], [resid, ho_own, *ho_parts], spot=False)
    d_qkv, n1_own, *sends = run(
        functools.partial(attend_back_kernel, n, docs),
        [out((length, 3 * group), bf16), block_f] + [block_l] * (n - 1),
        [doc_starts, *send_seq(pieces[0], pieces[1:]), qkv, lse, qkv_mat, cosine, sine],
        starts=1,
        scratch=[pltpu.VMEM((length, group), f32)] * 3
        + [pltpu.VMEM((length, group), bf16), pltpu.VMEM((length, width), f32)],
        flops=12 * length * width * group,
    )
    n1_parts = send_seq(n1_own, sends)
    (in_grad,) = run(
        functools.partial(input_back_kernel, n), [block_f], [*n1_parts, x, d_resid], spot=False
    )
    picked = [pltpu.VMEM((length, width // 2), bf16)]
    in_half = out((planes, strip, 3 * group), bf16)
    flops = 3 * length * width * group
    (send,) = run(grad_send_kernel, [in_half], [normed, d_qkv], scratch=picked, flops=flops)
    args = [normed, d_qkv, swap(send)]
    (in_sum,) = run(grad_all_kernel, [in_half], args, scratch=picked, flops=flops)
    in_sum = to_all(in_sum.reshape(planes * n, height, 3 * group))
    in_grads = run(
        functools.partial(sum_in_kernel, n), [out(w_query.shape, f32)] * 3, [in_sum], spot=False
    )
    keep, send = run(
        functools.partial(grad_out_kernel, n),
        [out((planes, height, width), f32), out((planes, height, width), bf16)],
        [*contexts, d_branch, *ho_parts],
        scratch=[
            pltpu.VMEM((width, length), f32),
            pltpu.VMEM((2 * planes * height, length), f32),
            pltpu.VMEM((length, width), bf16),
        ],
        flops=2 * length * group * width,
    )
    own, *sends = run(
        add_split_kernel,
        [out((height, width), f32)] + [out((height, width), bf16)] * (planes - 1),
        [keep, swap(send)],
    )
    parts = send_planes(own, sends)
    (grad_out,) = run(sum_kernel, [out(w_out.shape, f32)], parts, spot=False)
    return (
        hidden_out[None], in_grad[None], *in_grads, grad_out, grad_gate, grad_up, grad_down
    )


def solution(mesh):
    dp, seq = mesh.shape["dp"], mesh.shape["seq"]
    fine = Mesh(
        mesh.devices.reshape(dp // 2, 2, seq // 2, 2), ("plane", "core", "seq_hi", "seq_lo")
    )
    token = P(("plane", "core"), ("seq_hi", "seq_lo"), None)
    weight = P(("plane", "core", "seq_hi", "seq_lo"), None)
    return jax.shard_map(
        layer,
        mesh=fine,
        in_specs=(token, P(("plane", "core"), None)) + (weight,) * 7 + (token,),
        out_specs=(token, token) + (weight,) * 7,
        check_vma=False,
    )
```

```python
import functools
import typing

import jax
import jax.numpy as jnp
from jax import lax
from jax.experimental import pallas as pl
from jax.experimental.pallas import tpu as pltpu
from jax.sharding import Mesh, PartitionSpec as P


HEADS = 16
HEAD_DIM = 64
eps = 1e-05
bf16 = jnp.bfloat16
f32 = jnp.float32
NN = (((1,), (0,)), ((), ()))
NT = (((1,), (1,)), ((), ()))
TN = (((0,), (0,)), ((), ()))


def dot(left, right, dims=NN):
    return lax.dot_general(left, right, dims, preferred_element_type=f32)


def rows(start, size):
    return pl.ds(pl.multiple_of(start, size), size)


def norm_parts(values):
    centred = values - jnp.mean(values, axis=-1, keepdims=True)
    inv = lax.rsqrt(jnp.mean(centred * centred, axis=-1, keepdims=True) + eps)
    return centred * inv, inv


def norm_back(normed, inv, grad):
    mean_grad = jnp.mean(grad, axis=-1, keepdims=True)
    mean_both = jnp.mean(grad * normed, axis=-1, keepdims=True)
    return (grad - mean_grad - normed * mean_both) * inv


SEQ = ("seq_hi", "seq_lo")


def located(kernel, starts):
    def body(*refs):
        spot = [lax.axis_index(SEQ), lax.axis_index("plane"), lax.axis_index("core")]
        if starts:
            spot += [refs[0][0, t] for t in range(refs[0].shape[1])]
        kernel(spot, *refs[starts:])

    return body


def call(kernel, outs, args, scratch=(), flops=0, starts=0, spot=True, limit=24):
    vmem = pl.BlockSpec(memory_space=pltpu.VMEM)
    in_specs = [pl.BlockSpec(memory_space=pltpu.SMEM)] * starts + [vmem] * (len(args) - starts)
    moved = sum(a.size * a.dtype.itemsize for a in args) + sum(
        o.size * jnp.dtype(o.dtype).itemsize for o in outs
    )
    return pl.pallas_call(
        located(kernel, starts) if spot else kernel,
        out_shape=outs,
        in_specs=in_specs,
        out_specs=[vmem] * len(outs),
        scratch_shapes=list(scratch),
        cost_estimate=pl.CostEstimate(flops=flops, bytes_accessed=moved, transcendentals=0),
        compiler_params=pltpu.CompilerParams(vmem_limit_bytes=limit * 1024 * 1024),
    )(*args)


def out(shape, dtype):
    return jax.ShapeDtypeStruct(shape, dtype)


def turn(values, cosine, sine, sign):
    width = values.shape[-1]
    half = HEAD_DIM // 2
    lane = lax.broadcasted_iota(jnp.int32, values.shape, 1)
    first = (lane & (HEAD_DIM - 1)) < half
    ahead = pltpu.roll(values, width - half, 1)
    behind = pltpu.roll(values, half, 1)
    other = jnp.where(first, -ahead, behind)
    return values * cosine + (other * sine if sign > 0 else -(other * sine))


def head_lanes(shape, head):
    lane = lax.broadcasted_iota(jnp.int32, shape, 1)
    return (lane >= head * HEAD_DIM) & (lane < (head + 1) * HEAD_DIM)


def masked(scores, starts, first_row):
    pos = lax.broadcasted_iota(jnp.int32, (scores.shape[0], 1), 0) + first_row
    begin = jnp.zeros_like(pos)
    for start in starts:
        begin = jnp.where(pos >= start, start, begin)
    keys = lax.broadcasted_iota(jnp.int32, scores.shape, 1)
    return jnp.where((keys >= begin) & (keys <= pos), scores, -1e30)


def attend_kernel(d, docs, info, *refs):
    n = d.n
    count = 2 * sum(ways(d.planes))
    xs, blocks = refs[:n], refs[n : n + count]
    cos_ref, sin_ref, normed, mats, qkv, lse, context = refs[n + count :]
    j = info[0]
    tokens = xs[0].shape[0]
    for k in range(n):
        block, _ = norm_parts(xs[k][...].astype(f32))
        normed[rows((j ^ k) * tokens, tokens), :] = block.astype(bf16)

    def put(block, source):
        here = rows(block * d.strip, d.strip)
        for t in range(d.in_tiles):
            mats[here, t * 128 : (t + 1) * 128] = source[t * d.strip : (t + 1) * d.strip, :]

    each_block(d, info, blocks, put)
    pre = dot(normed[...], mats[...])
    width = pre.shape[1] // 3
    reps = width // cos_ref.shape[1]
    cosine = jnp.concatenate([cos_ref[...]] * reps, axis=1)
    sine = jnp.concatenate([sin_ref[...]] * reps, axis=1)
    qkv[:, :width] = (
        turn(pre[:, :width], cosine, sine, 1).astype(bf16).astype(f32) * HEAD_DIM**-0.5
    ).astype(bf16)
    qkv[:, width : 2 * width] = turn(pre[:, width : 2 * width], cosine, sine, 1).astype(bf16)
    qkv[:, 2 * width :] = pre[:, 2 * width :].astype(bf16)
    starts = [info[3 + d] for d in range(docs)]
    length = qkv.shape[0]
    step = 256

    for b in range(length // step):
        here, upto = slice(b * step, (b + 1) * step), slice(0, (b + 1) * step)
        query = qkv[here, :width]
        total = jnp.zeros((step, width), f32)
        for head in range(width // HEAD_DIM):
            mine = head_lanes(query.shape, head)
            scores = dot(jnp.where(mine, query, 0), qkv[upto, width : 2 * width], NT)
            scores = masked(scores, starts, b * step)
            top = jnp.max(scores, axis=-1, keepdims=True)
            expo = jnp.exp(scores - top)
            mass = jnp.sum(expo, axis=-1, keepdims=True)
            probs = (expo * (1.0 / mass)).astype(bf16)
            total = jnp.where(mine, dot(probs, qkv[upto, 2 * width :]), total)
            lse[here, head : head + 1] = top + jnp.log(mass)
        context[here, :] = total.astype(bf16)


class Dims(typing.NamedTuple):
    n: int
    planes: int
    height: int
    units: int
    slot: int
    width: int
    group: int

    @property
    def strip(self):
        return self.n * self.height

    @property
    def ff(self):
        return 2 * self.planes * self.slot

    @property
    def whole(self):
        return self.ff // 128 if self.shared else -(-self.ff // 128)

    @property
    def shared(self):
        return self.ff % 128 == 64

    @property
    def tiles(self):
        return 2 * self.whole + self.shared

    @property
    def wide(self):
        return (self.whole + self.shared) * 128

    @property
    def gu_rows(self):
        return self.tiles * self.strip

    @property
    def in_tiles(self):
        return 3 * self.group // 128

    @property
    def payload(self):
        return self.gu_rows + self.width // 128 * self.slot


def ways(planes):
    return (1, 1, 2, 2) if planes == 4 else (1,) * planes


def each_block(d, info, refs, place):
    z, c = info[1], info[2]
    outer = (z == 0) | (z == d.planes - 1)
    at = 0
    for k, count in enumerate(ways(d.planes)):
        for a in range(count):
            for m in range(2):
                put = functools.partial(place, 2 * (z ^ k) + (c ^ m), refs[at])
                at += 1
                if count == 1:
                    put()
                else:
                    pl.when(outer if a == 0 else jnp.logical_not(outer))(put)


def gate_up_tile(d, gate, up, t):
    if t < d.whole:
        return gate[:, t * 128 : (t + 1) * 128]
    if t < 2 * d.whole:
        return up[:, (t - d.whole) * 128 : (t - d.whole + 1) * 128]
    at = d.whole * 128
    return jnp.concatenate([gate[:, at : at + 64], up[:, at : at + 64]], axis=1)


def split_kernel(d, info, *refs):
    mats, (w_gate, w_up), pieces = refs[:3], refs[3:5], refs[5 : 5 + d.n]
    gate, up = refs[5 + d.n :]
    if d.slot > d.units:
        gate[...] = jnp.zeros_like(gate)
        up[...] = jnp.zeros_like(up)
    for group in range(d.n):
        for b in range(2 * d.planes):
            here = (b * d.n + group) * d.units
            there = slice(b * d.slot, b * d.slot + d.units)
            gate[:, there] = w_gate[:, here : here + d.units]
            up[:, there] = w_up[:, here : here + d.units]
        for k in range(d.n):

            @pl.when((info[0] ^ k) == group)
            def unused(group=group, k=k):
                for t in range(d.tiles):
                    tile = gate_up_tile(d, gate, up, t)
                    pieces[k][t * d.height : (t + 1) * d.height, :] = tile
                for t in range(d.in_tiles):
                    at = d.tiles + t
                    which, lane = divmod(t * 128, d.group)
                    lane += group * d.group
                    pieces[k][at * d.height : (at + 1) * d.height, :] = mats[which][
                        :, lane : lane + 128
                    ]


def place_kernel(d, info, *refs):
    pieces, (in_payload, gu_payload) = refs[: d.n], refs[d.n :]
    for k in range(d.n):
        for t in range(d.tiles + d.in_tiles):
            inner = t >= d.tiles
            at = (t - d.tiles if inner else t) * d.strip + (info[0] ^ k) * d.height
            piece = pieces[k][t * d.height : (t + 1) * d.height, :]
            (in_payload if inner else gu_payload)[rows(at, d.height), :] = piece


def join_kernel(d, info, *refs):
    pieces, (grad_gate, grad_up, gate, up) = refs[: d.n], refs[d.n :]
    for group in range(d.n):
        for k in range(d.n):

            @pl.when((info[0] ^ k) == group)
            def unused(k=k):
                for t in range(d.tiles):
                    tile = pieces[k][t * d.height : (t + 1) * d.height, :].astype(f32)
                    if t < d.whole:
                        gate[:, t * 128 : (t + 1) * 128] = tile
                    elif t < 2 * d.whole:
                        up[:, (t - d.whole) * 128 : (t - d.whole + 1) * 128] = tile
                    else:
                        gate[:, d.whole * 128 : d.whole * 128 + 64] = tile[:, :64]
                        up[:, d.whole * 128 : d.whole * 128 + 64] = tile[:, 64:]

        for b in range(2 * d.planes):
            there = (b * d.n + group) * d.units
            here = slice(b * d.slot, b * d.slot + d.units)
            grad_gate[:, there : there + d.units] = gate[:, here]
            grad_up[:, there : there + d.units] = up[:, here]


def out_mat_kernel(n, planes, info, *refs):
    parts, (whole,) = refs[:-1], refs[-1:]
    j, z, c = info[0], info[1], info[2]
    size = parts[0].shape[1]
    for p in range(n):
        for m in range(2):
            for k in range(planes):
                at = ((2 * (z ^ k) + (c ^ m)) * n + (j ^ p)) * size
                whole[rows(at, size), :] = parts[2 * p + m][k]


def project_kernel(n, info, *refs):
    contexts = refs[:n]
    mats = refs[n]
    xs = refs[n + 1 : 2 * n + 1]
    resid_own, normed, acc = refs[2 * n + 1 :]
    j = info[0]
    width = contexts[0].shape[1]
    tokens = xs[0].shape[0]
    acc[...] = dot(contexts[0][...], mats[rows(j * width, width), :])
    for p in range(1, n):
        acc[...] += dot(contexts[p][...], mats[rows((j ^ p) * width, width), :])
    for k in range(n):
        here = rows((j ^ k) * tokens, tokens)
        resid = xs[k][...].astype(f32) + acc[here, :]
        if k == 0:
            resid_own[...] = resid
        normed[here, :] = norm_parts(resid)[0].astype(bf16)


def gate_part(d, both):
    if d.shared:
        at = 2 * d.whole * 128
        return jnp.concatenate([both[:, : d.whole * 128], both[:, at:]], axis=1)
    return both[:, : d.whole * 128]


def up_part(d, both):
    at = d.whole * 128
    if d.shared:
        last = pltpu.roll(both[:, 2 * at :], 64, 1)
        return jnp.concatenate([both[:, at : 2 * at], last], axis=1)
    return both[:, at:]


def ffn_kernel(d, info, normed, *refs):
    count = 2 * sum(ways(d.planes))
    blocks, downs = refs[:count], refs[count : 2 * count]
    grads = refs[2 * count : 2 * count + d.n]
    hidden, d_gu, own_grad, *rest = refs[2 * count + d.n :]
    sends = rest[: d.n - 1]
    down_mat, og_full, gu_mat, acc = rest[d.n - 1 :]
    j = info[0]
    tokens = grads[0].shape[0]
    if d.slot > d.units:
        down_mat[...] = jnp.zeros_like(down_mat)
    elif d.wide > d.ff:
        down_mat[d.ff :, :] = jnp.zeros((d.wide - d.ff, d.width), bf16)

    def put_gu(block, source):
        here = rows(block * d.strip, d.strip)
        for t in range(d.tiles):
            gu_mat[here, t * 128 : (t + 1) * 128] = source[t * d.strip : (t + 1) * d.strip, :]

    def put_down(block, source):
        at = pl.multiple_of(block * d.slot, d.slot)
        down_mat[pl.ds(at, d.units), :] = source[...]

    each_block(d, info, blocks, put_gu)
    each_block(d, info, downs, put_down)
    for k in range(d.n):
        og_full[rows((j ^ k) * tokens, tokens), :] = grads[k][...]
    both = dot(normed[...], gu_mat[...])
    d_hidden = dot(og_full[...], down_mat[...], NT)
    gate, up = gate_part(d, both), up_part(d, both)
    sig = 1.0 / (1.0 + jnp.exp(-gate))
    silu = gate * sig
    mixed = silu * up
    d_gate = d_hidden * up * (sig + gate * sig * (1.0 - sig))
    d_up = d_hidden * silu
    at = d.whole * 128
    if d.shared:
        lane = lax.broadcasted_iota(jnp.int32, (mixed.shape[0], 128), 1)
        hidden[:, :at] = mixed[:, :at].astype(bf16)
        hidden[:, at:] = jnp.where(lane < 64, mixed[:, at:], 0.0).astype(bf16)
        last = jnp.where(lane < 64, d_gate[:, at:], pltpu.roll(d_up[:, at:], 64, 1))
        d_gu[:, 2 * at :] = last.astype(bf16)
    else:
        hidden[...] = mixed.astype(bf16)
    d_gu[:, :at] = d_gate[:, :at].astype(bf16)
    d_gu[:, at : 2 * at] = d_up[:, :at].astype(bf16)
    acc[...] = dot(d_gu[...], gu_mat[...], NT)
    own_grad[...] = acc[rows(j * tokens, tokens), :]
    for k in range(1, d.n):
        sends[k - 1][...] = acc[rows((j ^ k) * tokens, tokens), :].astype(bf16)


def hidden_out_kernel(n, info, left, right, resid, own, *rest):
    sends, acc = rest[:-1], rest[-1]
    j = info[0]
    tokens = own.shape[0]
    acc[...] = dot(left[...], right[...])
    own[...] = resid[...] + acc[rows(j * tokens, tokens), :]
    for k in range(1, n):
        sends[k - 1][...] = acc[rows((j ^ k) * tokens, tokens), :].astype(bf16)


def hidden_sum_kernel(own, *refs):
    total = own[...]
    for part in refs[:-1]:
        total = total + part[...].astype(f32)
    refs[-1][...] = total.astype(bf16)


def resid_back_kernel(n, info, *refs):
    parts = refs[:n]
    resid, out_grad, mats, d_resid, d_branch, *pieces, acc = refs[n:]
    grad = parts[0][...]
    for part in parts[1:]:
        grad = grad + part[...].astype(f32)
    normed, inv = norm_parts(resid[...])
    total = out_grad[...].astype(f32) + norm_back(normed, inv, grad)
    d_resid[...] = total
    d_branch[...] = total.astype(bf16)
    acc[...] = dot(total.astype(bf16), mats[...], NT)
    width = pieces[0].shape[1]
    for k in range(n):
        pieces[k][...] = acc[:, rows((info[0] ^ k) * width, width)].astype(bf16)


def input_back_kernel(n, *refs):
    parts = refs[:n]
    x, d_resid, in_grad = refs[n:]
    grad = parts[0][...]
    for part in parts[1:]:
        grad = grad + part[...].astype(f32)
    normed, inv = norm_parts(x[...].astype(f32))
    in_grad[...] = d_resid[...] + norm_back(normed, inv, grad)


def attend_back_kernel(n, docs, info, *refs):
    pieces = refs[:n]
    qkv, lse, mats, cos_ref, sin_ref = refs[n : n + 5]
    d_qkv, own, *rest = refs[n + 5 :]
    sends = rest[: n - 1]
    d_key, d_value, d_query, d_contexts, acc = rest[n - 1 :]
    j = info[0]
    tokens, width = pieces[0].shape
    for k in range(n):
        d_contexts[rows((j ^ k) * tokens, tokens), :] = pieces[k][...]
    length = qkv.shape[0]
    starts = [info[3 + d] for d in range(docs)]
    step = 256
    d_key[...] = jnp.zeros_like(d_key)
    d_value[...] = jnp.zeros_like(d_value)

    for b in range(length // step):
        here, upto = slice(b * step, (b + 1) * step), slice(0, (b + 1) * step)
        d_context = d_contexts[here, :]
        query = qkv[here, :width]
        keys = qkv[upto, width : 2 * width]
        d_q = jnp.zeros((step, width), f32)
        for head in range(width // HEAD_DIM):
            lanes = head_lanes(query.shape, head)
            q_head = jnp.where(lanes, query, 0)
            g_head = jnp.where(lanes, d_context, 0)
            scores = masked(dot(q_head, keys, NT), starts, b * step)
            probs = jnp.exp(scores - lse[here, head : head + 1])
            d_probs = dot(g_head, qkv[upto, 2 * width :], NT)
            delta = jnp.sum(probs * d_probs, axis=-1, keepdims=True)
            d_scores = (probs * (d_probs - delta)).astype(bf16)
            d_value[upto, :] += dot(probs.astype(bf16), g_head, TN)
            d_key[upto, :] += dot(d_scores, q_head, TN)
            d_q = jnp.where(lanes, dot(d_scores, keys), d_q)
        d_query[here, :] = d_q * HEAD_DIM**-0.5

    reps = width // cos_ref.shape[1]
    cosine = jnp.concatenate([cos_ref[...]] * reps, axis=1)
    sine = jnp.concatenate([sin_ref[...]] * reps, axis=1)
    low_q = d_query[...].astype(bf16).astype(f32)
    low_k = d_key[...].astype(bf16).astype(f32)
    d_qkv[:, :width] = turn(low_q, cosine, sine, -1).astype(bf16)
    d_qkv[:, width : 2 * width] = turn(low_k, cosine, sine, -1).astype(bf16)
    d_qkv[:, 2 * width :] = d_value[...].astype(bf16)
    acc[...] = dot(d_qkv[...], mats[...], NT)
    own[...] = acc[rows(j * tokens, tokens), :]
    for k in range(1, n):
        sends[k - 1][...] = acc[rows((j ^ k) * tokens, tokens), :].astype(bf16)


def pick_lanes(left, picked, core, planes):
    size = left.shape[1] // (2 * planes)
    for z in range(planes):
        if size % 128:
            low = left[:, 2 * z * size : (2 * z + 1) * size]
            high = left[:, (2 * z + 1) * size : (2 * z + 2) * size]
            picked[:, z * size : (z + 1) * size] = jnp.where(core == 0, low, high)
        else:
            picked[:, z * size : (z + 1) * size] = left[:, rows((2 * z + core) * size, size)]


def grad_send_kernel(info, left, right, send, picked):
    planes, size = send.shape[0], send.shape[1]
    pick_lanes(left, picked, 1 - info[2], planes)
    product = dot(picked[...], right[...], TN)
    for z in range(planes):
        send[z] = product[z * size : (z + 1) * size].astype(bf16)


def grad_all_kernel(info, left, right, got, total, picked):
    planes, size = got.shape[0], got.shape[1]
    pick_lanes(left, picked, info[2], planes)
    product = dot(picked[...], right[...], TN)
    for z in range(planes):
        total[z] = (product[z * size : (z + 1) * size] + got[z].astype(f32)).astype(bf16)


def parts_of(planes):
    return ((2, 3), (0, 1)) if planes == 4 else (tuple(range(1, planes)), (0,))


def pick_blocks(left, picked, core, z, ks):
    size = picked.shape[1] // len(ks)
    for at, k in enumerate(ks):
        if size % 128:
            both = left[:, rows((z ^ k) * 2 * size, 2 * size)]
            block = jnp.where(core == 0, both[:, :size], both[:, size:])
        else:
            block = left[:, rows((2 * (z ^ k) + core) * size, size)]
        picked[:, at * size : (at + 1) * size] = block


def ffn_send_kernel(d, ks, info, normed, d_gu, *refs):
    z, c = info[1], info[2]
    if len(refs) > 3:
        hidden, og_full, down, send, picked = refs
        down[...] = dot(hidden[...], og_full[...], TN)
    else:
        down, send, picked = refs
    pick_blocks(normed, picked, 1 - c, z, ks)
    product = dot(picked[...], d_gu[...], TN).astype(bf16)
    for at, k in enumerate(ks):
        for t in range(d.tiles):
            send[at, t * d.strip : (t + 1) * d.strip, :] = product[
                at * d.strip : (at + 1) * d.strip, t * 128 : (t + 1) * 128
            ]
        other = down[rows((2 * (z ^ k) + 1 - c) * d.slot, d.slot), :].astype(bf16)
        for t in range(d.width // 128):
            row = d.gu_rows + t * d.slot
            send[at, row : row + d.slot, :] = other[:, t * 128 : (t + 1) * 128]


def ffn_split_kernel(d, ks, info, normed, d_gu, down, got, *refs):
    outs, (picked, acc) = refs[:-2], refs[-2:]
    z, c = info[1], info[2]
    pick_blocks(normed, picked, c, z, ks)
    acc[...] = dot(picked[...], d_gu[...], TN)
    for at, k in enumerate(ks):
        mine = down[rows((2 * (z ^ k) + c) * d.slot, d.slot), :]
        for t in range(d.tiles):
            here, lanes = slice(t * d.strip, (t + 1) * d.strip), slice(t * 128, (t + 1) * 128)
            total = acc[at * d.strip : (at + 1) * d.strip, lanes] + got[at, here, :].astype(f32)
            if k:
                outs[at - len(ks)][here, :] = total.astype(bf16)
            else:
                outs[0][:, lanes] = total
        for t in range(d.width // 128):
            here = slice(d.gu_rows + t * d.slot, d.gu_rows + (t + 1) * d.slot)
            lanes = slice(t * 128, (t + 1) * 128)
            total = mine[:, lanes] + got[at, here, :].astype(f32)
            if k:
                outs[at - len(ks)][here, :] = total.astype(bf16)
            else:
                outs[1][:, lanes] = total


def ffn_mid_kernel(info, near, far, *refs):
    (first, second, third), (to_pair, to_mid) = refs[:3], refs[3:]
    inner = (info[1] == 1) | (info[1] == 2)
    passed = jnp.where(inner, second[...].astype(f32) + third[...].astype(f32), 0.0)
    to_pair[...] = (near[...].astype(f32) + passed).astype(bf16)
    to_mid[...] = (far[...].astype(f32) + first[...].astype(f32)).astype(bf16)


def ffn_sum_kernel(d, info, own_gu, own_down, *refs):
    count = 2 if d.planes == 4 else d.planes - 1
    parts = refs[:count]
    grad_down, *pieces, acc = refs[count:]
    inner = (info[1] == 1) | (info[1] == 2)

    def add(total, here):
        for k, part in enumerate(parts):
            block = part[here, :].astype(f32)
            total = total + (jnp.where(inner, block, 0.0) if k and d.planes == 4 else block)
        return total

    for t in range(d.tiles):
        acc[...] = add(own_gu[:, t * 128 : (t + 1) * 128], slice(t * d.strip, (t + 1) * d.strip))
        for k in range(d.n):
            pieces[k][t * d.height : (t + 1) * d.height, :] = acc[
                rows((info[0] ^ k) * d.height, d.height), :
            ].astype(bf16)
    for t in range(d.width // 128):
        at, lanes = d.gu_rows + t * d.slot, slice(t * 128, (t + 1) * 128)
        grad_down[:, lanes] = add(own_down[: d.units, lanes], slice(at, at + d.units))


def add_split_kernel(info, keep, got, own, *sends):
    z = info[1]
    own[...] = keep[z] + got[z].astype(f32)
    for k in range(1, keep.shape[0]):
        sends[k - 1][...] = (keep[z ^ k] + got[z ^ k].astype(f32)).astype(bf16)


def sum_kernel(*refs):
    total = refs[0][...]
    for part in refs[1:-1]:
        total = total + part[...].astype(f32)
    refs[-1][...] = total


def sum_in_kernel(n, parts, *grads):
    planes = parts.shape[0] // n
    width = parts.shape[2] // 3
    for group in range(n):
        total = parts[group].astype(f32)
        for z in range(1, planes):
            total = total + parts[z * n + group].astype(f32)
        for t in range(3):
            grads[t][:, group * width : (group + 1) * width] = total[:, t * width : (t + 1) * width]


def grad_out_kernel(n, info, *refs):
    contexts, branches = refs[:n], refs[n : 2 * n]
    keep, send, turned, left, right = refs[2 * n :]
    j, c = info[0], info[2]
    width = contexts[0].shape[1]
    tokens = branches[0].shape[0]
    for p in range(n):
        right[rows((j ^ p) * tokens, tokens), :] = branches[p][...]
        turned[rows((j ^ p) * width, width), :] = contexts[p][...].astype(f32).T
    planes, height = keep.shape[0], keep.shape[1]
    block = height * n
    for m in range(2):
        for z in range(planes):
            at = (2 * z + (c ^ m)) * block + j * height
            left[pl.ds((m * planes + z) * height, height), :] = turned[
                pl.ds(pl.multiple_of(at, height), height), :
            ]
    product = dot(left[...].astype(bf16), right[...])
    for z in range(planes):
        keep[z] = product[z * height : (z + 1) * height]
        send[z] = product[(planes + z) * height : (planes + z + 1) * height].astype(bf16)


MIDDLE = ((2, 4), (3, 5), (4, 2), (5, 3), (0, 1), (1, 0), (6, 7), (7, 6))
LAST = tuple((2 * a + t, 2 * b + t) for a, b in ((1, 3), (2, 0), (0, 1), (3, 2)) for t in range(2))
FIRST = tuple((b, a) for a, b in LAST)


def layer(hidden_in, doc_starts, w_query, w_key, w_value, w_out, w_gate, w_up, w_down, out_grad):
    x = hidden_in[0]
    og = out_grad[0]
    tokens, width = x.shape
    seq = SEQ
    n = lax.axis_size(seq)
    planes = lax.axis_size("plane")
    length = tokens * n
    group = HEADS // n * HEAD_DIM
    docs = doc_starts.shape[1]
    height = w_query.shape[0]
    strip = n * height
    units = w_down.shape[0]
    slot = units if units % 8 == 0 else -(-units // 16) * 16
    d = Dims(n, planes, height, units, slot, width, group)
    z = lax.axis_index("plane")

    def swap(a):
        return lax.ppermute(a, "core", [(0, 1), (1, 0)])

    def around(a, k):
        return lax.ppermute(a, seq, [(t, t ^ k) for t in range(n)])

    def across(a, k):
        return lax.ppermute(a, "plane", [(t, t ^ k) for t in range(planes)])

    def gather_seq(a):
        return [a] + [around(a, k) for k in range(1, n)]

    def between(a, pairs):
        return lax.ppermute(a, ("plane", "core"), pairs)

    def gather_planes(a):
        if planes != 4:
            return [(a,)] + [(across(a, k),) for k in range(1, planes)]
        pair = across(a, 1)
        mid = between(a, MIDDLE)
        far = across(mid, 1)
        near = between(pair, MIDDLE)
        last = between(pair, LAST)
        return [(a,), (pair,), (far, near), (last, mid)]

    def both_cores(blocks):
        return [b for ways in blocks for a in ways for b in (a, swap(a))]

    def send_seq(own, sends):
        return [own] + [around(a, k + 1) for k, a in enumerate(sends)]

    def send_planes(own, sends):
        return [own] + [across(a, k + 1) for k, a in enumerate(sends)]

    def to_all(blocks):
        axes = ("plane",) + seq
        return lax.all_to_all(blocks, axes, split_axis=0, concat_axis=0, tiled=True)

    def run(kernel, outs, args, **kw):
        return call(kernel, outs, args, **kw)

    half = HEAD_DIM // 2
    freq = 10000.0 ** (-(jnp.arange(half, dtype=f32) * 2.0) / HEAD_DIM)
    lane_freq = jnp.concatenate([freq] * (128 // half))
    angle = jnp.arange(length, dtype=f32)[:, None] * lane_freq[None, :]
    cosine, sine = jnp.cos(angle), jnp.sin(angle)

    out_rows = gather_planes(w_out)
    pieces = run(
        functools.partial(split_kernel, d),
        [out(((d.tiles + d.in_tiles) * height, 128), bf16)] * n,
        [w_query, w_key, w_value, w_gate, w_up],
        scratch=[pltpu.VMEM((height, d.wide), bf16)] * 2,
        limit=60,
    )
    in_payload, gu_payload = run(
        functools.partial(place_kernel, d),
        [out((d.in_tiles * strip, 128), bf16), out((d.gu_rows, 128), bf16)],
        send_seq(pieces[0], pieces[1:]),
    )
    xs = gather_seq(x)
    in_blocks = both_cores(gather_planes(in_payload))
    gu_blocks = both_cores(gather_planes(gu_payload))
    row_blocks = both_cores(gather_planes(w_down))
    ogs = gather_seq(og)
    outer = (z == 0) | (z == planes - 1)
    out_planes = jnp.stack(
        [
            jnp.where(outer, a[0], a[1]) if len(a) > 1 else a[0] for a in out_rows
        ]
    )
    out_parts = [b for a in gather_seq(out_planes) for b in (a, swap(a))]
    (out_mat,) = run(
        functools.partial(out_mat_kernel, n, planes), [out((width, width), bf16)], [*out_parts]
    )

    normed, qkv_mat, qkv, lse, context = run(
        functools.partial(attend_kernel, d, docs),
        [
            out((length, width), bf16),
            out((width, 3 * group), bf16),
            out((length, 3 * group), bf16),
            out((length, HEADS // n), f32),
            out((length, group), bf16),
        ],
        [doc_starts, *xs, *in_blocks, cosine, sine],
        starts=1,
        flops=8 * length * width * group,
    )
    contexts = gather_seq(context)
    resid, normed2 = run(
        functools.partial(project_kernel, n),
        [out((tokens, width), f32), out((length, width), bf16)],
        [*contexts, out_mat, *xs],
        scratch=[pltpu.VMEM((length, width), f32)],
        flops=2 * length * width * width,
    )
    block_f = out((tokens, width), f32)
    block_l = out((tokens, width), bf16)
    cols = d.tiles * 128
    hidden, d_gu, dn_own, *rest = run(
        functools.partial(ffn_kernel, d),
        [out((length, d.wide), bf16), out((length, cols), bf16), block_f]
        + [block_l] * (n - 1)
        + [out((d.wide, width), bf16), out((length, width), bf16)],
        [normed2, *gu_blocks, *row_blocks, *ogs],
        scratch=[pltpu.VMEM((width, cols), bf16), pltpu.VMEM((length, width), f32)],
        flops=10 * length * width * d.ff,
    )
    dn_parts = send_seq(dn_own, rest[: n - 1])
    down_mat, og_full = rest[n - 1 :]

    down_grads, sent, outs = None, [], []
    for part, ks in enumerate(parts_of(planes)):
        payload = out((len(ks), d.payload, 128), bf16)
        args = [normed2, d_gu, down_grads] if part else [normed2, d_gu, hidden, og_full]
        *made, send = run(
            functools.partial(ffn_send_kernel, d, ks),
            [payload] if part else [out((d.wide, width), f32), payload],
            args,
            scratch=[pltpu.VMEM((length, len(ks) * strip), bf16)],
            flops=2 * length * len(ks) * strip * cols + (0 if part else 2 * length * d.ff * width),
        )
        down_grads = made[0] if made else down_grads
        sent.append(swap(send))
    for part, ks in enumerate(parts_of(planes)):
        owned = [out((strip, cols), f32), out((slot, width), f32)] if 0 in ks else []
        outs.append(
            run(
                functools.partial(ffn_split_kernel, d, ks),
                owned + [out((d.payload, 128), bf16)] * sum(k > 0 for k in ks),
                [normed2, d_gu, down_grads, sent[part]],
                scratch=[
                    pltpu.VMEM((length, len(ks) * strip), bf16),
                    pltpu.VMEM((len(ks) * strip, cols), f32),
                ],
                flops=2 * length * len(ks) * strip * cols,
            )
        )
    own_gu, own_down, *near = outs[1]
    sends = [*near, *outs[0]]
    if planes == 4:
        near, two, far = sends
        parts = [across(two, 1), between(two, MIDDLE), between(far, FIRST)]
        to_pair, to_mid = run(
            ffn_mid_kernel, [out((d.payload, 128), bf16)] * 2, [near, far, *parts]
        )
        ffn_parts = [across(to_pair, 1), between(to_mid, MIDDLE)]
    else:
        ffn_parts = [across(a, k + 1) for k, a in enumerate(sends)]
    grad_down, *pieces = run(
        functools.partial(ffn_sum_kernel, d),
        [out(w_down.shape, f32)] + [out((d.tiles * height, 128), bf16)] * n,
        [own_gu, own_down, *ffn_parts],
        scratch=[pltpu.VMEM((strip, 128), f32)],
    )
    grad_gate, grad_up = run(
        functools.partial(join_kernel, d),
        [out(w_gate.shape, f32)] * 2,
        [*send_seq(pieces[0], pieces[1:])],
        scratch=[pltpu.VMEM((height, d.wide), f32)] * 2,
    )

    d_resid, d_branch, *pieces = run(
        functools.partial(resid_back_kernel, n),
        [block_f, block_l] + [out((tokens, group), bf16)] * n,
        [*dn_parts, resid, og, out_mat],
        scratch=[pltpu.VMEM((tokens, width), f32)],
        flops=2 * tokens * width * width,
    )
    ho_own, *sends = run(
        functools.partial(hidden_out_kernel, n),
        [block_f] + [block_l] * (n - 1),
        [hidden, down_mat, resid],
        scratch=[pltpu.VMEM((length, width), f32)],
        flops=2 * length * width * d.ff,
    )
    (hidden_out,) = run(hidden_sum_kernel, [block_l], send_seq(ho_own, sends), spot=False)
    branches = gather_seq(d_branch)
    d_qkv, n1_own, *sends = run(
        functools.partial(attend_back_kernel, n, docs),
        [out((length, 3 * group), bf16), block_f] + [block_l] * (n - 1),
        [doc_starts, *send_seq(pieces[0], pieces[1:]), qkv, lse, qkv_mat, cosine, sine],
        starts=1,
        scratch=[pltpu.VMEM((length, group), f32)] * 3
        + [pltpu.VMEM((length, group), bf16), pltpu.VMEM((length, width), f32)],
        flops=12 * length * width * group,
    )
    n1_parts = send_seq(n1_own, sends)
    (in_grad,) = run(
        functools.partial(input_back_kernel, n), [block_f], [*n1_parts, x, d_resid], spot=False
    )
    picked = [pltpu.VMEM((length, width // 2), bf16)]
    in_half = out((planes, strip, 3 * group), bf16)
    flops = 3 * length * width * group
    (send,) = run(grad_send_kernel, [in_half], [normed, d_qkv], scratch=picked, flops=flops)
    args = [normed, d_qkv, swap(send)]
    (in_sum,) = run(grad_all_kernel, [in_half], args, scratch=picked, flops=flops)
    in_sum = to_all(in_sum.reshape(planes * n, height, 3 * group))
    in_grads = run(
        functools.partial(sum_in_kernel, n), [out(w_query.shape, f32)] * 3, [in_sum], spot=False
    )
    keep, send = run(
        functools.partial(grad_out_kernel, n),
        [out((planes, height, width), f32), out((planes, height, width), bf16)],
        [*contexts, *branches],
        scratch=[
            pltpu.VMEM((width, length), f32),
            pltpu.VMEM((2 * planes * height, length), f32),
            pltpu.VMEM((length, width), bf16),
        ],
        flops=2 * length * group * width,
    )
    own, *sends = run(
        add_split_kernel,
        [out((height, width), f32)] + [out((height, width), bf16)] * (planes - 1),
        [keep, swap(send)],
    )
    parts = send_planes(own, sends)
    (grad_out,) = run(sum_kernel, [out(w_out.shape, f32)], parts, spot=False)
    return (
        hidden_out[None], in_grad[None], *in_grads, grad_out, grad_gate, grad_up, grad_down
    )


def solution(mesh):
    dp, seq = mesh.shape["dp"], mesh.shape["seq"]
    fine = Mesh(
        mesh.devices.reshape(dp // 2, 2, seq // 2, 2), ("plane", "core", "seq_hi", "seq_lo")
    )
    token = P(("plane", "core"), ("seq_hi", "seq_lo"), None)
    weight = P(("plane", "core", "seq_hi", "seq_lo"), None)
    return jax.shard_map(
        layer,
        mesh=fine,
        in_specs=(token, P(("plane", "core"), None)) + (weight,) * 7 + (token,),
        out_specs=(token, token) + (weight,) * 7,
        check_vma=False,
    )
```
